256 devices in a mesh: dp: 32 (over y, z), mp: 8 (over x, core).
Axes of the slice: x: 4, y: 4, z: 8, core: 2. Of those that a mesh axis runs over, the one named last changes fastest.
Arguments:
- hidden_act: bfloat16 [8192, 14336], P('dp', 'mp'), may hold values from -6 to 6
- readout: bfloat16 [8192, 2560], P('dp'), may hold values from -6 to 6
- log_gap: float32 [1024, 8], P('dp'), may hold values from -0.6 to 0.6
- advantage: float32 [1024], P('dp'), may hold values from -6 to 6
- version: int32 [1024], P('dp'), may hold values from 0 to 3
- lengths: int32 [32, 32], P('dp'), may hold values from 1 to 8, 224 in all within a row
- routes: int32 [1024, 1], P('dp'), may hold values from 0 to 31; in each aligned block of 32 rows (0 to 31, 32 to 63, ...) at most 2 rows name the same one
- weight: bfloat16 [14336, 2560], P(('mp', 'dp')), may hold values from -0.046875 to 0.046875
Outputs:
- log_ratio: float32 [2048, 8], P('dp')
- weight_grad: float32 [14336, 2560], P(('mp', 'dp'))
The draws below stay inside these ranges and needn't reach their ends.
Inputs may be any that keep to these rules, and one draw needn't show every extreme that they name: `routes`: among the 32 responses of one generator device at most 2 name the same learner shard, and some shard receives exactly 2; every learner shard receives at least one response. The lengths of one generator device's responses sum to 224, and one of them is 8.
All inputs are finite; a program needn't handle non-finite values.
Results may differ from the reference program's by a relative error of at most 0.0029.
Values may be sent and summed in bfloat16 or wider, within the bound.
A program may use at most 64 MiB of HBM per device.

```python
import math
import jax
import jax.numpy as jnp
import numpy as np
from jax import lax

D = 2560
FF = 14336
SEG = 8
R = 32
NVER = 4
N_DP = 32


def plant(array, rng, least, high):
    longest = array.shape.index(max(array.shape))
    spots = []
    for shift in (0, 1):
        where = [jax.random.randint(jax.random.fold_in(rng, axis), (), 0, length) for axis, length in enumerate(array.shape)]
        where[longest] = (where[longest] + shift) % array.shape[longest]
        spots.append(tuple(where))
    return array.at[spots[0]].set(least).at[spots[1]].set(high)


def steps_of(rng, dims, split, smallest, largest):
    def one(dim, blocks):
        heights = jax.random.uniform(jax.random.fold_in(jax.random.fold_in(rng, 6), dim), (blocks,), jnp.float32, smallest / len(split), largest / len(split))
        return jnp.repeat(jnp.exp(heights), dims[dim] // blocks).reshape((-1,) + (1,) * (len(dims) - dim - 1))

    factor_of = one(*split[0])
    for cut in split[1:]:
        factor_of = factor_of * one(*cut)
    return factor_of


def length_profile(number_of, total, reach, lean):
    portions = [(1 << 20) // math.isqrt(rank ** lean) + 1 for rank in range(2, number_of + 1)]
    spare, given = total - reach - (number_of - 1), [1] * (number_of - 1)
    while spare > 0:
        free = [i for i in range(number_of - 1) if given[i] < reach]
        pool, remaining = sum([portions[i] for i in free]), spare
        for i in free:
            extra = min(reach - given[i], max(1, remaining * portions[i] // pool), spare)
            given[i] = given[i] + extra
            spare = spare - extra
    return np.array([reach] + given)


def ragged(key, amount, total, limit, skew):
    if amount == 2:
        one = jax.random.randint(key, (), max(1, total - limit), min(limit, total - 1) + 1)
        return jnp.stack([one, total - one])
    tallies = jnp.asarray(length_profile(amount, total, limit, skew), jnp.int32)
    twos = (amount - 1) // 2
    giver, taker = tallies[1:1 + 2 * twos:2], tallies[2:2 + 2 * twos:2]
    margin = jnp.minimum(giver - 1, limit - taker)
    shifted = jax.random.randint(jax.random.fold_in(key, 1), (twos,), 0, 1 << 20) % (margin + 1)
    tallies = tallies.at[1:1 + 2 * twos:2].set(giver - shifted).at[2:2 + 2 * twos:2].set(taker + shifted)
    return tallies[jax.random.permutation(jax.random.fold_in(key, 2), amount)]


def deal_out(key, own, number, rows, count, top, bound, lean):
    sequence = jax.random.permutation(key, count)
    heavy_load, ordinary = load_shares(count, rows * top, bound, lean, True), load_shares(count, rows * top, bound, lean, False)
    places = jnp.arange(count)

    def named(sizes, turn):
        used = int((sizes > 0).sum())
        fixed = max(1, used // 4)
        moved = fixed + (places - fixed + turn * (used - fixed)) % max(1, count - fixed)
        return jnp.zeros((count,), jnp.int32).at[sequence[jnp.where(places < fixed, places, moved)]].set(jnp.asarray(sizes, jnp.int32))

    sizes = jnp.where(number % 4 == 0, named(heavy_load, number // 4), named(ordinary, number - number // 4 - 1))
    mixed = jax.random.permutation(jax.random.fold_in(own, 3), count)
    donor, taker = mixed[0:count // 2 * 2:2], mixed[1:count // 2 * 2:2]
    margin = jnp.minimum(sizes[donor] - 1, bound - sizes[taker]) // 2
    margin = jnp.where((donor == sequence[0]) | (taker == sequence[0]) | (sizes[taker] == 0), 0, jnp.maximum(margin, 0))
    moved = jax.random.randint(jax.random.fold_in(own, 4), (count // 2,), 0, 1 << 20) % (margin + 1)
    sizes = sizes.at[donor].add(-moved).at[taker].add(moved)
    items = jnp.searchsorted(jnp.cumsum(sizes), jnp.arange(rows * top), side="right").astype(jnp.int32)
    table = items.reshape(top, rows).T
    table = table[jax.random.permutation(jax.random.fold_in(own, 1), rows)]
    turn = jax.random.randint(jax.random.fold_in(own, 2), (rows, 1), 0, top)
    return jnp.take_along_axis(table, (jnp.arange(top)[None, :] + turn) % top, axis=1)


def load_shares(number_of, total, reach, lean, full):
    portions = [(1 << 20) // math.isqrt(rank ** lean) + 1 for rank in range(1, number_of + 1)]
    largest = reach if full else min(reach, max(-(-total // number_of), total * portions[0] // sum(portions)))
    least = 1 if total - largest >= number_of - 1 else 0
    given, spare = [largest] + [least] * (number_of - 1), total - largest - least * (number_of - 1)
    while spare > 0:
        free = [i for i in range(1, number_of) if given[i] < largest] or [i for i in range(1, number_of) if given[i] < reach]
        pool, remaining = sum([portions[i] for i in free]), spare
        for i in free:
            addition = min(reach - given[i], max(1, remaining * portions[i] // pool), spare)
            given[i] = given[i] + addition
            spare = spare - addition
    return np.array(given)


def scatter_about(own_key, dims, deviation, most, split=(), kind=jnp.bfloat16):
    drawn = deviation * jax.random.normal(own_key, dims, jnp.float32)
    if split:
        drawn = drawn * steps_of(own_key, dims, split, -0.22, 0.18)
    return jnp.clip(drawn, -most, most).astype(kind)


def setup_inputs(seed: int = 0) -> dict:
    arg_keys = jax.random.split(jax.random.key(seed), 9)
    hidden_act = scatter_about(arg_keys[0], (N_DP * R * SEG, FF), 1.0, 6.0, ((0, 32), (1, 8)))
    readout = scatter_about(arg_keys[1], (N_DP * R * SEG, D), 1.0, 6.0, ((0, 32),))
    log_gap = scatter_about(arg_keys[2], (N_DP * R, SEG), 0.1, 0.6, ((0, 32),), jnp.float32)
    advantage = scatter_about(arg_keys[3], (N_DP * R,), 1.0, 6.0, ((0, 32),), jnp.float32)
    version = plant(jax.random.randint(arg_keys[4], (N_DP * R,), 0, NVER), jax.random.fold_in(arg_keys[4], 1), 0, NVER - 1).astype(jnp.int32)
    lengths = jax.vmap(lambda own: ragged(own, R, 7 * R * SEG // 8, SEG, 2))(jax.random.split(arg_keys[5], N_DP)).reshape((N_DP, R)).astype(jnp.int32)
    routes_keys = jax.random.split(jax.random.fold_in(arg_keys[6], 1), (N_DP * R) // R)
    routes_turns = jax.random.permutation(jax.random.fold_in(arg_keys[6], 3), (N_DP * R) // R)
    routes = jax.vmap(lambda own, number: deal_out(jax.random.fold_in(arg_keys[6], 2), own, number, R, N_DP, 1, 2 * R // N_DP, 2))(routes_keys, routes_turns).reshape((N_DP * R, 1))
    weight = scatter_about(arg_keys[7], (FF, D), FF ** -0.5, 0.046875, ((0, 256),))
    return {"hidden_act": hidden_act, "readout": readout, "log_gap": log_gap, "advantage": advantage, "version": version, "lengths": lengths, "routes": routes, "weight": weight}


def reference(hidden_act, readout, log_gap, advantage, version, lengths, routes, weight):
    slots = 2 * R // N_DP
    layer_out = jnp.dot(hidden_act, weight, preferred_element_type=jnp.float32)
    shift = 0.15 / math.sqrt(D) * lax.optimization_barrier(jnp.sum(layer_out * readout.astype(jnp.float32), axis=1))
    logit_all = log_gap + shift.reshape(N_DP * R, SEG)
    lens = lengths.reshape(-1)
    positions = jnp.arange(SEG, dtype=jnp.int32)
    live = positions[None, :] < lens[:, None]
    dest = routes[:, 0]
    onehot = (dest.reshape(N_DP, R)[:, :, None] == jnp.arange(N_DP, dtype=jnp.int32)[None, None, :]).astype(jnp.int32)
    rank = lax.optimization_barrier(jnp.sum((jnp.cumsum(onehot, axis=1) - onehot) * onehot, axis=2)).reshape(-1)
    source = jnp.arange(N_DP * R, dtype=jnp.int32) // R
    flat_hot = onehot.reshape(N_DP * R, N_DP).astype(jnp.float32)
    shard_count = lax.optimization_barrier(jnp.sum(flat_hot * lens.astype(jnp.float32)[:, None], axis=0))
    count_each = lax.optimization_barrier(jnp.sum(flat_hot * shard_count[None, :], axis=1))
    slot_index = ((dest * N_DP + source) * slots + rank).astype(jnp.int32)
    log_ratio = jnp.zeros((N_DP * N_DP * slots, SEG), jnp.float32).at[slot_index].set(jnp.where(live, logit_all, 0.0))
    stale = jnp.power(jnp.float32(0.7), (NVER - 1 - version).astype(jnp.float32))
    ratio = jnp.exp(logit_all)
    squash = jnp.tanh((ratio - 1.0) / 0.2)
    clipped = 1.0 + 0.2 * squash
    adv = advantage[:, None]
    plain = ratio * adv <= clipped * adv
    slope = jnp.where(plain, 1.0, 1.0 - squash * squash)
    coef = jnp.where(live, -512.0 * stale[:, None] * adv * ratio * slope / count_each[:, None], 0.0)
    out_grad = (coef.reshape(-1)[:, None] * (0.15 / math.sqrt(D)) * readout.astype(jnp.float32)).astype(jnp.bfloat16)
    weight_grad = lax.dot_general(hidden_act, out_grad, (((0,), (0,)), ((), ())), preferred_element_type=jnp.float32)
    return (log_ratio, weight_grad)
```

```python
import functools
import math

import jax
import jax.numpy as jnp
from jax import lax
from jax.experimental import pallas as pl
from jax.experimental.pallas import tpu as pltpu
from jax.sharding import PartitionSpec as P

MESH = pl.DeviceIdType.MESH
BF = jnp.bfloat16
F32 = jnp.float32

NX, NY, NZ = 4, 4, 8
TOK = 256
DH = 1280
ROWS = 56
FB = ROWS * NZ
FALL = 2 * FB
CH = 256
NCH = DH // CH
NSEM = 140


def hdot(a, b):
    return lax.dot_general(
        a, b, (((1,), (0,)), ((), ())), precision=lax.Precision.HIGHEST,
        preferred_element_type=F32,
    )


def iota(shape, dim):
    return lax.broadcasted_iota(jnp.int32, shape, dim)


def kernel(scale_out, h_in, r_in, w_in, gap_ref, adv_ref, ver_ref, len_ref, route_ref,
           lr_out, g_out,
           wbuf, wcat, rbuf, hv, htr, ht, relay, pkf, kb, ar1, ar2, lb, og, gbuf,
           rss, rsr, stage, local_sem, send_sem, recv_sem):
    dp = lax.axis_index("dp")
    mp = lax.axis_index("mp")
    y, z = dp // NZ, dp % NZ
    x, c = mp // 2, mp % 2
    px = x % 2
    o = 1 - c
    yp, ym, y2 = (y + 1) % NY, (y + 3) % NY, (y + 2) % NY
    zp, zm = (z + 1) % NZ, (z + 7) % NZ
    xp, xm = (x + 1) % NX, (x + 3) % NX

    def dev(yy, zz, xx, cc):
        return (yy * NZ + zz, xx * 2 + cc)

    d_yp, d_ym, d_y2 = dev(yp, z, x, c), dev(ym, z, x, c), dev(y2, z, x, c)
    d_zp, d_zm = dev(y, zp, x, c), dev(y, zm, x, c)
    d_xp, d_xm = dev(y, z, xp, c), dev(y, z, xm, c)
    d_co = dev(y, z, x, o)

    count = [0]
    sent = []

    def send(src, dst, where):
        n = count[0]
        count[0] += 1
        copy = pltpu.make_async_remote_copy(
            src_ref=src, dst_ref=dst, send_sem=send_sem.at[n], recv_sem=recv_sem.at[n],
            device_id=where, device_id_type=MESH,
        )
        copy.start()
        sent.append(copy)
        return copy

    half = pl.ds(pl.multiple_of(c * DH, 128), DH)
    other = pl.ds(pl.multiple_of(o * DH, 128), DH)
    mine = pl.ds(pl.multiple_of(y * TOK, TOK), TOK)
    cp_h = pltpu.make_async_copy(h_in, hv, local_sem.at[0])
    cp_h.start()
    cp_r = pltpu.make_async_copy(r_in.at[:, half], rbuf.at[mine, :], local_sem.at[1])
    cp_r.start()
    cp_w = pltpu.make_async_copy(w_in.at[:, half], wbuf.at[c, z], local_sem.at[2])
    cp_w.start()

    barrier = pltpu.get_barrier_semaphore()
    greet = [d_zp, d_zm, d_yp, d_ym, d_y2]
    greet += [(dp, (mp + k) % 8) for k in range(1, 8)]
    for where in greet:
        pl.semaphore_signal(barrier, inc=1, device_id=where, device_id_type=MESH)
    pl.semaphore_wait(barrier, len(greet))

    W = {}
    w_own = w_in.at[:, half]
    w_co = send(w_in.at[:, other], wbuf.at[c, z], d_co)
    W[0, 0, 1] = send(w_own, wbuf.at[c, z], d_zp)
    W[0, 1, 1] = send(w_own, wbuf.at[c, z], d_zm)

    hb = px * 128

    def rows_in(part):
        return pl.ds(pl.multiple_of(hb + part * 64, 64), 64)

    def rows_at(yy, part):
        return pl.ds(pl.multiple_of(yy * TOK + hb + part * 64, 64), 64)

    def r_first(part, where):
        return send(r_in.at[rows_in(part), half], rbuf.at[rows_at(y, part), :], where)

    rp_a = r_first(0, d_yp)
    rm_b = r_first(1, d_ym)
    rp_b = r_first(1, d_yp)
    rm_a = r_first(0, d_ym)

    cp_h.wait()
    for j in range(7):
        htr[j * 256:(j + 1) * 256, :] = hv[:, j * 256:(j + 1) * 256].T

    def h_rows(yy, first, rows):
        return pl.ds(pl.multiple_of(yy * FB + first, 32), rows)

    def cols_at(yy):
        return pl.ds(pl.multiple_of(yy * TOK, TOK), TOK)

    h2p = send(htr.at[h_rows(y2, 0, FB // 2), :], relay.at[0], d_yp)
    h2m = send(htr.at[h_rows(y2, FB // 2, FB // 2), :], relay.at[1], d_ym)

    w_co.wait_recv()
    W[1, 0, 1] = send(wbuf.at[o, z], wbuf.at[o, z], d_zp)
    W[1, 1, 1] = send(wbuf.at[o, z], wbuf.at[o, z], d_zm)

    cp_ho = pltpu.make_async_copy(
        htr.at[h_rows(y, 0, FB), :], ht.at[c, :, cols_at(y)], local_sem.at[3])
    cp_ho.start()

    dest_b = jnp.broadcast_to(route_ref[...].astype(F32), (32, 32))
    ri, ci = iota((32, 32), 0), iota((32, 32), 1)
    dest_row = jnp.sum(jnp.where(ri == ci, dest_b, 0.0), axis=0, keepdims=True)
    earlier = jnp.where((dest_b == dest_row) & (ri < ci), 1.0, 0.0)
    rank_row = jnp.sum(earlier, axis=0, keepdims=True)
    key_row = dest_row * 2.0 + rank_row
    ver = ver_ref[...]
    stale_row = jnp.where(
        ver == 3, 1.0, jnp.where(ver == 2, 0.7, jnp.where(ver == 1, 0.7 ** 2, 0.7 ** 3))
    ).astype(F32)
    row8, resp8 = iota((8, 32), 0), iota((8, 32), 1)
    mine8 = (row8 // 2 == y) & (resp8 // 16 == row8 % 2)
    spread = jnp.where(iota((32, 128), 0) % 16 == iota((32, 128), 1) // 8, 1.0, 0.0)

    def lay(v):
        return hdot(jnp.where(mine8, jnp.broadcast_to(v, (8, 32)), 0.0), spread)

    tile = jnp.where(iota((8, 128), 0) == iota((8, 128), 1) % 8, 1.0, 0.0)
    gap_wide = hdot(gap_ref[...], tile) * spread
    own_rows = iota((8, 128), 0) // 2 == y
    position = (iota((8, 128), 1) % 8).astype(F32)
    len_t = lay(len_ref[...].astype(F32))
    pkf[y, 0] = hdot(jnp.where(mine8, 1.0, 0.0), gap_wide)
    pkf[y, 1] = jnp.where(own_rows & (position >= len_t), -1.0, lay(key_row))
    pkf[y, 2] = lay(adv_ref[...])
    pkf[y, 3] = lay(stale_row)
    pk = [send(pkf.at[y], pkf.at[y], d) for d in (d_yp, d_ym, d_y2)]

    def w_forward(k, s):
        core = c if k == 0 else o
        for d, where in ((0, d_zp), (1, d_zm)):
            W[k, d, s].wait_recv()
            origin = (z + (8 - s if d == 0 else s)) % NZ
            if s < 3:
                ref = wbuf.at[core, origin]
            else:
                ref = wbuf.at[core, origin, :, d * (DH // 2):(d + 1) * (DH // 2)]
            W[k, d, s + 1] = send(ref, ref, where)

    w_forward(0, 1)

    def along(ref_rows, where):
        ref = rbuf.at[ref_rows, :]
        return send(ref, ref, where)

    rp_a.wait_recv()
    r2a = along(rows_at(ym, 0), d_yp)
    xa = [along(rows_at(ym, 0), d_xm)]
    rm_b.wait_recv()
    r2b = along(rows_at(yp, 1), d_ym)
    xb = [along(rows_at(yp, 1), d_xp)]

    h1p = send(htr.at[h_rows(yp, 0, FB), :], ht.at[c, :, cols_at(y)], d_yp)
    h1m = send(htr.at[h_rows(ym, 0, FB), :], ht.at[c, :, cols_at(y)], d_ym)
    cp_ho.wait()
    hp = [send(ht.at[c, :, cols_at(y)], ht.at[c, :, cols_at(y)], d_co)]

    w_forward(1, 1)

    rp_b.wait_recv()
    xb.append(along(rows_at(ym, 1), d_xp))
    rm_a.wait_recv()
    xa.append(along(rows_at(yp, 0), d_xm))

    for copy in pk:
        copy.wait_recv()
    fields = [pkf[0, f] + pkf[1, f] + pkf[2, f] + pkf[3, f] for f in range(4)]
    kb[z] = fields[1]
    K = {}
    K[0, 1] = send(kb.at[z], kb.at[z], d_zp)
    K[1, 1] = send(kb.at[z], kb.at[z], d_zm)

    def ring_forward(table, buf, s):
        for d, where in ((0, d_zp), (1, d_zm)):
            if (d, s) not in table:
                continue
            table[d, s].wait_recv()
            if s + 1 > (4 if d == 0 else 3):
                continue
            origin = (z + (8 - s if d == 0 else s)) % NZ
            table[d, s + 1] = send(buf.at[origin], buf.at[origin], where)

    w_forward(0, 2)

    h2p.wait_recv()
    hq_p = send(relay.at[0], ht.at[c, 0:FB // 2, cols_at(ym)], d_yp)
    h2m.wait_recv()
    hq_m = send(relay.at[1], ht.at[c, FB // 2:FB, cols_at(yp)], d_ym)

    w_forward(1, 2)
    ring_forward(K, kb, 1)

    r2a.wait_recv()
    xa.append(along(rows_at(y2, 0), d_xm))
    r2b.wait_recv()
    xb.append(along(rows_at(y2, 1), d_xp))

    w_forward(0, 3)

    h1p.wait_recv()
    hp.append(send(ht.at[c, :, cols_at(ym)], ht.at[c, :, cols_at(ym)], d_co))
    h1m.wait_recv()
    hp.append(send(ht.at[c, :, cols_at(yp)], ht.at[c, :, cols_at(yp)], d_co))

    w_forward(1, 3)
    ring_forward(K, kb, 2)

    hq_p.wait_recv()
    hq_m.wait_recv()
    hp.append(send(ht.at[c, :, cols_at(y2)], ht.at[c, :, cols_at(y2)], d_co))

    cp_r.wait()
    cp_w.wait()
    for copy in xa + xb:
        copy.wait_recv()
    for k in range(2):
        for d in range(2):
            W[k, d, 4].wait_recv()
    ring_forward(K, kb, 3)
    for copy in hp:
        copy.wait_recv()

    for core in range(2):
        for j in range(NZ // 2):
            for n in range(NCH):
                cols = slice(n * CH, (n + 1) * CH)
                pair = jnp.concatenate(
                    [wbuf[core, 2 * j, :, cols].astype(F32),
                     wbuf[core, 2 * j + 1, :, cols].astype(F32)], axis=0)
                first = core * FB + 2 * j * ROWS
                wcat[first:first + 2 * ROWS, cols] = pair.astype(BF)
    parts = []
    for b in range(NY):
        u = lax.dot_general(
            wcat[...], rbuf[b * TOK:(b + 1) * TOK, :], (((1,), (1,)), ((), ())),
            preferred_element_type=F32,
        )
        h = ht[:, :, b * TOK:(b + 1) * TOK].reshape(FALL, TOK).astype(F32)
        s = jnp.sum(u * h, axis=0, keepdims=True)
        parts += [s[:, 0:128], s[:, 128:256]]
    ar1[mp] = jnp.concatenate(parts, axis=0)
    first_stage = [
        send(ar1.at[mp], ar1.at[mp], (dp, (mp + k) % 8)) for k in range(1, 8)
    ]
    ring_forward(K, kb, 4)

    keys = [jnp.floor(kb[i] * 0.5) for i in range(NZ)]
    own_dest = jnp.floor(fields[1] * 0.5)
    count_each = jnp.ones((8, 128), F32)
    for k in range(NY * NZ):
        hits = jnp.zeros((8, 128), F32)
        for i in range(NZ):
            hits = hits + jnp.where(keys[i] == float(k), 1.0, 0.0)
        total = jnp.sum(jnp.sum(hits, axis=0, keepdims=True), axis=1, keepdims=True)
        count_each = jnp.where(own_dest == float(k), jnp.broadcast_to(total, (8, 128)), count_each)

    for copy in first_stage:
        copy.wait_recv()
    acc = ar1[0]
    for i in range(1, 8):
        acc = acc + ar1[i]
    ar2[y] = acc
    second_stage = [send(ar2.at[y], ar2.at[y], d) for d in (d_yp, d_ym, d_y2)]
    for copy in second_stage:
        copy.wait_recv()
    total = (ar2[0] + ar2[1]) + (ar2[2] + ar2[3])

    gap, key, adv, stale = fields
    live = key >= 0.0
    logit = gap + total * scale_out
    lb[z] = jnp.where(live, logit, 0.0)
    ratio = jnp.exp(logit)
    squash = jnp.tanh((ratio - 1.0) / 0.2)
    clipped = 1.0 + 0.2 * squash
    plain = ratio * adv <= clipped * adv
    slope = jnp.where(plain, 1.0, 1.0 - squash * squash)
    coef = jnp.where(live, -512.0 * stale * adv * ratio * slope / count_each, 0.0)
    coef_col = (coef * scale_out).T

    RS = {}

    def push(d, s, n, cols, where):
        RS[d, s, n] = send(rss.at[d, s - 1, n, :, :, cols], rsr.at[d, s - 1, n, :, :, cols], where)

    ends = ((0, d_zp), (1, d_zm))
    sides = (slice(0, CH // 2), slice(CH // 2, CH))
    far = (z + 4) % NZ
    hall = ht[...].reshape(FALL, NY * TOK)
    for n in range(NCH):
        cols = slice(n * CH, (n + 1) * CH)
        for b in range(8):
            rows = slice(b * 128, (b + 1) * 128)
            og[rows, cols] = (coef_col[:, b:b + 1] * rbuf[rows, cols].astype(F32)).astype(BF)
        g = jnp.dot(hall, og[:, cols], preferred_element_type=F32)
        gbuf[n] = g.reshape(2, NZ, ROWS, CH)
        for d, where in ends:
            rss[d, 0, n, :, :, sides[d]] = gbuf[n, :, far, :, sides[d]].astype(BF)
            push(d, 1, n, sides[d], where)

    L = {}
    L[0, 1] = send(lb.at[z], lb.at[z], d_zp)
    L[1, 1] = send(lb.at[z], lb.at[z], d_zm)

    full = slice(0, CH)
    for s in range(2, 5):
        for n in range(NCH):
            for d, where in ends:
                to = (z + (5 - s if d == 0 else 3 + s)) % NZ
                RS[d, s - 1, n].wait_recv()
                if s == 2:
                    a, b = sides[d], sides[1 - d]
                    rss[d, 1, n, :, :, a] = (
                        gbuf[n, :, to, :, a] + rsr[d, 0, n, :, :, a].astype(F32)).astype(BF)
                    rss[d, 1, n, :, :, b] = gbuf[n, :, to, :, b].astype(BF)
                else:
                    rss[d, s - 1, n] = (
                        gbuf[n, :, to] + rsr[d, s - 2, n].astype(F32)).astype(BF)
                push(d, s, n, full, where)
        ring_forward(L, lb, s - 1)

    last = []
    for n in range(NCH):
        for d, _ in ends:
            RS[d, 4, n].wait_recv()
        cols = pl.ds(pl.multiple_of(c * DH + n * CH, CH), CH)
        stage[n] = gbuf[n, o, z] + rsr[0, 3, n, o].astype(F32) + rsr[1, 3, n, o].astype(F32)
        last.append(send(stage.at[n], g_out.at[:, cols], d_co))
        g_out[:, cols] = gbuf[n, c, z] + rsr[0, 3, n, c].astype(F32) + rsr[1, 3, n, c].astype(F32)

    ring_forward(L, lb, 4)
    key_all = kb[...].reshape(64, 128)
    val_all = lb[...].reshape(64, 128)
    fold = jnp.where(iota((128, 8), 0) % 8 == iota((128, 8), 1), 1.0, 0.0)
    oi, ki = iota((64, 64), 0), iota((64, 64), 1)
    source = ((ki % 8) // 2) * NZ + ki // 8
    out = jnp.zeros((64, 8), F32)
    for r in range(2):
        want = (2 * dp + r).astype(F32)
        v = hdot(jnp.where(key_all == want, val_all, 0.0), fold)
        out = out + hdot(jnp.where(oi == 2 * source + r, 1.0, 0.0), v)
    lr_out[...] = out

    for copy in last:
        copy.wait_recv()
    for copy in sent:
        copy.wait_send()


def body(hidden_act, readout, log_gap, advantage, version, lengths, routes, weight):
    width = readout.shape[1]
    any_spec = pl.BlockSpec(memory_space=pl.ANY)
    vmem = pl.BlockSpec(memory_space=pltpu.VMEM)
    return tuple(pl.pallas_call(
        functools.partial(kernel, 0.15 / math.sqrt(width)),
        out_shape=(
            jax.ShapeDtypeStruct((64, 8), F32),
            jax.ShapeDtypeStruct((ROWS, 2 * DH), F32),
        ),
        in_specs=[any_spec] * 3 + [vmem] * 5,
        out_specs=(vmem, vmem),
        scratch_shapes=[
            pltpu.VMEM((2, NZ, ROWS, DH), BF),
            pltpu.VMEM((FALL, DH), BF),
            pltpu.VMEM((NY * TOK, DH), BF),
            pltpu.VMEM((TOK, 4 * FB), BF),
            pltpu.VMEM((4 * FB, TOK), BF),
            pltpu.VMEM((2, FB, NY * TOK), BF),
            pltpu.VMEM((2, FB // 2, TOK), BF),
            pltpu.VMEM((NY, 4, 8, 128), F32),
            pltpu.VMEM((NZ, 8, 128), F32),
            pltpu.VMEM((8, 8, 128), F32),
            pltpu.VMEM((NY, 8, 128), F32),
            pltpu.VMEM((NZ, 8, 128), F32),
            pltpu.VMEM((NY * TOK, DH), BF),
            pltpu.VMEM((NCH, 2, NZ, ROWS, CH), F32),
            pltpu.VMEM((2, 4, NCH, 2, ROWS, CH), BF),
            pltpu.VMEM((2, 4, NCH, 2, ROWS, CH), BF),
            pltpu.VMEM((NCH, ROWS, CH), F32),
            pltpu.SemaphoreType.DMA((4,)),
            pltpu.SemaphoreType.DMA((NSEM,)),
            pltpu.SemaphoreType.DMA((NSEM,)),
        ],
        compiler_params=pltpu.CompilerParams(
            collective_id=0, has_side_effects=True, vmem_limit_bytes=60 * 1024 * 1024,
        ),
    )(hidden_act, readout, weight, log_gap, advantage.reshape(1, -1), version.reshape(1, -1),
      lengths, routes))


def solution(mesh):
    placed = (
        P("dp", "mp"),
        P("dp", None),
        P("dp", None),
        P("dp"),
        P("dp"),
        P("dp", None),
        P("dp", None),
        P(("mp", "dp"), None),
    )
    return jax.shard_map(
        body,
        mesh=mesh,
        in_specs=placed,
        out_specs=(P("dp", None), P(("mp", "dp"), None)),
        check_vma=False,
    )
```

```python
import functools
import math

import jax
import jax.numpy as jnp
from jax import lax
from jax.experimental import pallas as pl
from jax.experimental.pallas import tpu as pltpu
from jax.sharding import PartitionSpec as P

MESH = pl.DeviceIdType.MESH
BF = jnp.bfloat16
F32 = jnp.float32

NX, NY, NZ = 4, 4, 8
TOK = 256
DH = 1280
ROWS = 56
FB = ROWS * NZ
FALL = 2 * FB
CH = 256
NCH = DH // CH
NSEM = 190


def hdot(a, b):
    return lax.dot_general(
        a, b, (((1,), (0,)), ((), ())), precision=lax.Precision.HIGHEST,
        preferred_element_type=F32,
    )


def iota(shape, dim):
    return lax.broadcasted_iota(jnp.int32, shape, dim)


def kernel(scale_out, h_in, r_in, w_in, gap_in, adv_in, ver_in, len_in, route_in,
           lr_out, g_out,
           gap_ref, adv_ref, ver_ref, len_ref, route_ref, lr_buf,
           wbuf, wfar, wcat, ubuf, rbuf, hv, htr, ht, relay, pkf, kb, ar1, ar2, lb, og, gbuf,
           rss, rsr, pown, stage, local_sem, send_sem, recv_sem):
    dp = lax.axis_index("dp")
    mp = lax.axis_index("mp")
    y, z = dp // NZ, dp % NZ
    x, c = mp // 2, mp % 2
    px = x % 2
    o = 1 - c
    yp, ym, y2 = (y + 1) % NY, (y + 3) % NY, (y + 2) % NY
    zp, zm = (z + 1) % NZ, (z + 7) % NZ
    xp, xm = (x + 1) % NX, (x + 3) % NX

    def dev(yy, zz, xx, cc):
        return (yy * NZ + zz, xx * 2 + cc)

    d_yp, d_ym, d_y2 = dev(yp, z, x, c), dev(ym, z, x, c), dev(y2, z, x, c)
    d_zp, d_zm = dev(y, zp, x, c), dev(y, zm, x, c)
    d_xp, d_xm = dev(y, z, xp, c), dev(y, z, xm, c)
    d_co = dev(y, z, x, o)
    d_zp_o, d_zm_o = dev(y, zp, x, o), dev(y, zm, x, o)

    count = [0]
    sent = []

    def send(src, dst, where):
        n = count[0]
        count[0] += 1
        copy = pltpu.make_async_remote_copy(
            src_ref=src, dst_ref=dst, send_sem=send_sem.at[n], recv_sem=recv_sem.at[n],
            device_id=where, device_id_type=MESH,
        )
        copy.start()
        sent.append(copy)
        return copy

    half = pl.ds(pl.multiple_of(c * DH, 128), DH)
    other = pl.ds(pl.multiple_of(o * DH, 128), DH)
    mine = pl.ds(pl.multiple_of(y * TOK, TOK), TOK)
    cp_h = pltpu.make_async_copy(h_in, hv, local_sem.at[0])
    cp_h.start()
    cp_r = pltpu.make_async_copy(r_in.at[:, half], rbuf.at[mine, :], local_sem.at[1])
    cp_r.start()
    cp_w = pltpu.make_async_copy(w_in.at[:, half], wbuf.at[c, z], local_sem.at[2])
    cp_w.start()

    small = []
    for i, (a, b) in enumerate((
            (gap_in, gap_ref), (adv_in, adv_ref), (ver_in, ver_ref), (len_in, len_ref),
            (route_in, route_ref))):
        small.append(pltpu.make_async_copy(a, b, local_sem.at[4 + i]))
        small[-1].start()

    far = (z + 4) % NZ
    for core in range(2):
        wbuf[core, far] = jnp.zeros((ROWS, DH), BF)

    barrier = pltpu.get_barrier_semaphore()
    chips = [(dp, (mp + k) % 8) for k in range(1, 8)]
    greet = [d_zp, d_zm, d_zp_o, d_zm_o, d_yp, d_ym, d_y2] + chips
    for where in greet:
        pl.semaphore_signal(barrier, inc=1, device_id=where, device_id_type=MESH)
    pl.semaphore_wait(barrier, len(greet))

    W = {}
    WH = DH // 2
    order = ((0, 0), (1, 1), (0, 1), (1, 0))

    def w_first(k, d, h, where):
        first = (c if k == 0 else o) * DH + h * WH
        return send(
            w_in.at[:, pl.ds(pl.multiple_of(first, 128), WH)],
            wbuf.at[c, z, :, h * WH:(h + 1) * WH], where)

    for d, h in order:
        W[0, h, d, 1] = w_first(0, d, h, (d_zp, d_zm)[d])

    hb = px * 128

    def rows_in(part):
        return pl.ds(pl.multiple_of(hb + part * 64, 64), 64)

    def rows_at(yy, part):
        return pl.ds(pl.multiple_of(yy * TOK + hb + part * 64, 64), 64)

    def r_first(part, where):
        return send(r_in.at[rows_in(part), half], rbuf.at[rows_at(y, part), :], where)

    rp_a = r_first(0, d_yp)
    rm_b = r_first(1, d_ym)
    for d, h in order:
        W[1, h, d, 1] = w_first(1, d, h, (d_zp_o, d_zm_o)[d])
    w_co = send(w_in.at[:, other], wbuf.at[c, z], d_co)

    cp_h.wait()
    for j in range(7):
        htr[j * 256:(j + 1) * 256, :] = hv[:, j * 256:(j + 1) * 256].T

    def h_rows(yy, first, rows):
        return pl.ds(pl.multiple_of(yy * FB + first, 32), rows)

    def cols_at(yy):
        return pl.ds(pl.multiple_of(yy * TOK, TOK), TOK)

    h2p = send(htr.at[h_rows(y2, 0, FB // 2), :], relay.at[0], d_yp)
    h2m = send(htr.at[h_rows(y2, FB // 2, FB // 2), :], relay.at[1], d_ym)

    rp_b = r_first(1, d_yp)
    rm_a = r_first(0, d_ym)

    cp_ho = pltpu.make_async_copy(
        htr.at[h_rows(y, 0, FB), :], ht.at[c, :, cols_at(y)], local_sem.at[3])
    cp_ho.start()

    for copy in small:
        copy.wait()
    dest_row = route_ref[...].astype(F32)
    ri, ci = iota((32, 32), 0), iota((32, 32), 1)
    dest_col = jnp.sum(
        jnp.where(ri == ci, jnp.broadcast_to(dest_row, (32, 32)), 0.0), axis=1, keepdims=True)
    earlier = jnp.where((dest_col == dest_row) & (ri < ci), 1.0, 0.0)
    rank_row = jnp.sum(earlier, axis=0, keepdims=True)
    key_row = dest_row * 2.0 + rank_row
    ver = ver_ref[...]
    stale_row = jnp.where(
        ver == 3, 1.0, jnp.where(ver == 2, 0.7, jnp.where(ver == 1, 0.7 ** 2, 0.7 ** 3))
    ).astype(F32)
    row8, resp8 = iota((8, 32), 0), iota((8, 32), 1)
    mine8 = (row8 // 2 == y) & (resp8 // 16 == row8 % 2)
    spread = jnp.where(iota((32, 128), 0) % 16 == iota((32, 128), 1) // 8, 1.0, 0.0)

    def lay(v):
        return hdot(jnp.where(mine8, jnp.broadcast_to(v, (8, 32)), 0.0), spread)

    tile = jnp.where(iota((8, 128), 0) == iota((8, 128), 1) % 8, 1.0, 0.0)
    gap_wide = lax.dot_general(
        gap_ref[...], tile, (((0,), (0,)), ((), ())), precision=lax.Precision.HIGHEST,
        preferred_element_type=F32) * spread
    own_rows = iota((8, 128), 0) // 2 == y
    position = (iota((8, 128), 1) % 8).astype(F32)
    len_t = lay(len_ref[...].astype(F32))
    pkf[y, 0] = hdot(jnp.where(mine8, 1.0, 0.0), gap_wide)
    pkf[y, 1] = jnp.where(own_rows & (position >= len_t), -1.0, lay(key_row))
    pkf[y, 2] = lay(adv_ref[...])
    pkf[y, 3] = lay(stale_row)
    pk = [send(pkf.at[y], pkf.at[y], d) for d in (d_yp, d_ym, d_y2)]

    def w_forward(k, s):
        core = c if k == 0 else o
        for d, h in order:
            W[k, h, d, s].wait_recv()
            if s == 3 and h != d:
                continue
            origin = (z + (8 - s if d == 0 else s)) % NZ
            cols = slice(h * WH, (h + 1) * WH)
            src = wbuf.at[core, origin, :, cols]
            dst = src if s < 3 else wfar.at[core, :, cols]
            W[k, h, d, s + 1] = send(src, dst, (d_zp, d_zm)[d])

    w_forward(0, 1)

    def along(ref_rows, where):
        ref = rbuf.at[ref_rows, :]
        return send(ref, ref, where)

    rp_a.wait_recv()
    r2a = along(rows_at(ym, 0), d_yp)
    xa = [along(rows_at(ym, 0), d_xm)]
    rm_b.wait_recv()
    r2b = along(rows_at(yp, 1), d_ym)
    xb = [along(rows_at(yp, 1), d_xp)]

    cp_ho.wait()
    hp = [send(ht.at[c, :, cols_at(y)], ht.at[c, :, cols_at(y)], d_co)]

    w_forward(1, 1)

    h2p.wait_recv()
    hq_p = send(relay.at[0], ht.at[c, 0:FB // 2, cols_at(ym)], d_yp)
    h2m.wait_recv()
    hq_m = send(relay.at[1], ht.at[c, FB // 2:FB, cols_at(yp)], d_ym)
    h1 = []
    for first in (0, FB // 2):
        rows = slice(first, first + FB // 2)
        for to, where in ((yp, d_yp), (ym, d_ym)):
            h1.append(send(
                htr.at[h_rows(to, first, FB // 2), :], ht.at[c, rows, cols_at(y)], where))

    for copy in pk:
        copy.wait_recv()
    fields = [pkf[0, f] + pkf[1, f] + pkf[2, f] + pkf[3, f] for f in range(4)]
    kb[z] = fields[1]
    K = {}
    K[0, 1] = send(kb.at[z], kb.at[z], d_zp)
    K[1, 1] = send(kb.at[z], kb.at[z], d_zm)

    def ring_forward(table, buf, s):
        for d, where in ((0, d_zp), (1, d_zm)):
            if (d, s) not in table:
                continue
            table[d, s].wait_recv()
            if s + 1 > (4 if d == 0 else 3):
                continue
            origin = (z + (8 - s if d == 0 else s)) % NZ
            table[d, s + 1] = send(buf.at[origin], buf.at[origin], where)

    w_forward(0, 2)

    rp_b.wait_recv()
    xb.append(along(rows_at(ym, 1), d_xp))
    rm_a.wait_recv()
    xa.append(along(rows_at(yp, 0), d_xm))
    ring_forward(K, kb, 1)

    w_forward(1, 2)

    r2a.wait_recv()
    xa.append(along(rows_at(y2, 0), d_xm))
    r2b.wait_recv()
    xb.append(along(rows_at(y2, 1), d_xp))

    ring_forward(K, kb, 2)
    w_forward(0, 3)

    hq_p.wait_recv()
    hq_m.wait_recv()
    hp.append(send(ht.at[c, :, cols_at(y2)], ht.at[c, :, cols_at(y2)], d_co))

    w_forward(1, 3)
    ring_forward(K, kb, 3)

    cp_w.wait()
    w_co.wait_recv()
    for core in range(2):
        for j in range(NZ // 2):
            for n in range(NCH):
                cols = slice(n * CH, (n + 1) * CH)
                pair = jnp.concatenate(
                    [wbuf[core, 2 * j, :, cols].astype(F32),
                     wbuf[core, 2 * j + 1, :, cols].astype(F32)], axis=0)
                first = core * FB + 2 * j * ROWS
                wcat[first:first + 2 * ROWS, cols] = pair.astype(BF)

    def contract(w, r):
        return lax.dot_general(w, r, (((1,), (1,)), ((), ())), preferred_element_type=F32)

    def block(yy):
        ubuf[yy] = contract(wcat[...], rbuf[pl.ds(pl.multiple_of(yy * TOK, TOK), TOK), :])

    cp_r.wait()
    block(y)
    for copy in (xa[0], xb[0], xa[1], xb[1]):
        copy.wait_recv()
    block(ym)
    block(yp)
    for i in range(2):
        rows = slice(i * (FB // 2), (i + 1) * (FB // 2))
        for j, yy in ((0, ym), (1, yp)):
            h1[2 * i + j].wait_recv()
            ref = ht.at[c, rows, cols_at(yy)]
            hp.append(send(ref, ref, d_co))
    xa[2].wait_recv()
    xb[2].wait_recv()
    block(y2)
    ring_forward(K, kb, 4)

    keys = [jnp.floor(kb[i] * 0.5) for i in range(NZ)]
    own_dest = jnp.floor(fields[1] * 0.5)
    count_each = jnp.ones((8, 128), F32)
    for k in range(NY * NZ):
        hits = jnp.zeros((8, 128), F32)
        for i in range(NZ):
            hits = hits + jnp.where(keys[i] == float(k), 1.0, 0.0)
        total = jnp.sum(jnp.sum(hits, axis=0, keepdims=True), axis=1, keepdims=True)
        count_each = jnp.where(own_dest == float(k), jnp.broadcast_to(total, (8, 128)), count_each)

    for k in range(2):
        for d in range(2):
            W[k, d, d, 4].wait_recv()
    shifted = far % 2 == 1
    first = pl.multiple_of(far * ROWS - 8 * (far % 2), 16)
    for copy in hp:
        copy.wait_recv()
    total = jnp.zeros((1, NY * TOK), F32)
    pad = jnp.zeros((8, DH), F32)
    for core in range(2):
        w = wfar[core].astype(F32)
        w = jnp.where(shifted, jnp.concatenate([pad, w], 0), jnp.concatenate([w, pad], 0))
        u = contract(w.astype(BF), rbuf[...])
        total = total + jnp.sum(
            u * ht[core, pl.ds(first, 64), :].astype(F32), axis=0, keepdims=True)
    parts = []
    for b in range(NY):
        h = ht[:, :, b * TOK:(b + 1) * TOK].reshape(FALL, TOK).astype(F32)
        s = total[:, b * TOK:(b + 1) * TOK] + jnp.sum(ubuf[b] * h, axis=0, keepdims=True)
        parts += [s[:, 0:128], s[:, 128:256]]
    ar1[mp] = jnp.concatenate(parts, axis=0)
    partial = [send(ar1.at[mp], ar1.at[mp], where) for where in chips]

    for copy in partial:
        copy.wait_recv()
    ar2[y] = ((ar1[0] + ar1[1]) + (ar1[2] + ar1[3])) + ((ar1[4] + ar1[5]) + (ar1[6] + ar1[7]))
    partial = [send(ar2.at[y], ar2.at[y], where) for where in (d_yp, d_ym, d_y2)]
    for copy in partial:
        copy.wait_recv()
    total = (ar2[0] + ar2[1]) + (ar2[2] + ar2[3])

    gap, key, adv, stale = fields
    live = key >= 0.0
    logit = gap + total * scale_out
    lb[z] = jnp.where(live, logit, 0.0)
    ratio = jnp.exp(logit)
    squash = jnp.tanh((ratio - 1.0) / 0.2)
    clipped = 1.0 + 0.2 * squash
    plain = ratio * adv <= clipped * adv
    slope = jnp.where(plain, 1.0, 1.0 - squash * squash)
    coef = jnp.where(live, -512.0 * stale * adv * ratio * slope / count_each, 0.0)
    coef_col = (coef * scale_out).T

    RS = {}

    def push(d, s, n, cols, where):
        RS[d, s, n] = send(rss.at[d, s - 1, n, :, :, cols], rsr.at[d, s - 1, n, :, :, cols], where)

    ends = ((0, d_zp), (1, d_zm))
    sides = (slice(0, CH // 2), slice(CH // 2, CH))
    hall = ht[...].reshape(FALL, NY * TOK)
    for n in range(NCH):
        cols = slice(n * CH, (n + 1) * CH)
        for b in range(8):
            rows = slice(b * 128, (b + 1) * 128)
            og[rows, cols] = (coef_col[:, b:b + 1] * rbuf[rows, cols].astype(F32)).astype(BF)
        g = jnp.dot(hall, og[:, cols], preferred_element_type=F32)
        gbuf[n] = g.reshape(2, NZ, ROWS, CH)
        for d, where in ends:
            rss[d, 0, n, :, :, sides[d]] = gbuf[n, :, far, :, sides[d]].astype(BF)
            push(d, 1, n, sides[d], where)
    shares = [send(gbuf.at[n, o, z], pown.at[n], d_co) for n in range(NCH)]

    L = {}
    L[0, 1] = send(lb.at[z], lb.at[z], d_zp)
    L[1, 1] = send(lb.at[z], lb.at[z], d_zm)

    full = slice(0, CH)
    for s in range(2, 5):
        for n in range(NCH):
            for d, where in ends:
                to = (z + (5 - s if d == 0 else 3 + s)) % NZ
                RS[d, s - 1, n].wait_recv()
                if s == 2:
                    a, b = sides[d], sides[1 - d]
                    rss[d, 1, n, :, :, a] = (
                        gbuf[n, :, to, :, a] + rsr[d, 0, n, :, :, a].astype(F32)).astype(BF)
                    rss[d, 1, n, :, :, b] = gbuf[n, :, to, :, b].astype(BF)
                else:
                    rss[d, s - 1, n] = (
                        gbuf[n, :, to] + rsr[d, s - 2, n].astype(F32)).astype(BF)
                if s < 4:
                    push(d, s, n, full, where)
                else:
                    RS[d, 4, n] = [
                        send(rss.at[d, 3, n, c], rsr.at[d, 3, n, 0], where),
                        send(rss.at[d, 3, n, o], rsr.at[d, 3, n, 1], (d_zp_o, d_zm_o)[d]),
                    ]
        ring_forward(L, lb, s - 1)

    ring_forward(L, lb, 4)
    key_all = kb[...].reshape(64, 128)
    val_all = lb[...].reshape(64, 128)
    fold = jnp.where(iota((128, 8), 0) % 8 == iota((128, 8), 1), 1.0, 0.0)
    oi, ki = iota((64, 64), 0), iota((64, 64), 1)
    source = ((ki % 8) // 2) * NZ + ki // 8
    out = jnp.zeros((64, 8), F32)
    for r in range(2):
        want = (2 * dp + r).astype(F32)
        v = hdot(jnp.where(key_all == want, val_all, 0.0), fold)
        out = out + hdot(jnp.where(oi == 2 * source + r, 1.0, 0.0), v)
    lr_buf[...] = out.T
    outs = [pltpu.make_async_copy(lr_buf, lr_out, local_sem.at[9])]
    outs[0].start()

    for n in range(NCH):
        shares[n].wait_recv()
        for d, _ in ends:
            for copy in RS[d, 4, n]:
                copy.wait_recv()
        stage[0, n] = gbuf[n, c, z] + rsr[0, 3, n, 0].astype(F32) + rsr[1, 3, n, 0].astype(F32)
        stage[1, n] = pown[n] + rsr[0, 3, n, 1].astype(F32) + rsr[1, 3, n, 1].astype(F32)
        for i, core in enumerate((c, o)):
            cols = pl.ds(pl.multiple_of(core * DH + n * CH, CH), CH)
            out = pltpu.make_async_copy(
                stage.at[i, n], g_out.at[:, cols], local_sem.at[10 + 2 * n + i])
            out.start()
            outs.append(out)

    for copy in outs:
        copy.wait()
    for copy in sent:
        copy.wait_send()
    assert count[0] <= NSEM, count[0]


def body(hidden_act, readout, log_gap, advantage, version, lengths, routes, weight):
    width = readout.shape[1]
    any_spec = pl.BlockSpec(memory_space=pl.ANY)
    vmem = pl.BlockSpec(memory_space=pltpu.VMEM)
    lr, grad = pl.pallas_call(
        functools.partial(kernel, 0.15 / math.sqrt(width)),
        out_shape=(
            jax.ShapeDtypeStruct((8, 64), F32),
            jax.ShapeDtypeStruct((ROWS, 2 * DH), F32),
        ),
        in_specs=[any_spec] * 8,
        out_specs=(any_spec, any_spec),
        scratch_shapes=[
            pltpu.VMEM((8, 32), F32),
            pltpu.VMEM((1, 32), F32),
            pltpu.VMEM((1, 32), jnp.int32),
            pltpu.VMEM((1, 32), jnp.int32),
            pltpu.VMEM((1, 32), jnp.int32),
            pltpu.VMEM((8, 64), F32),
            pltpu.VMEM((2, NZ, ROWS, DH), BF),
            pltpu.VMEM((2, ROWS, DH), BF),
            pltpu.VMEM((FALL, DH), BF),
            pltpu.VMEM((NY, FALL, TOK), F32),
            pltpu.VMEM((NY * TOK, DH), BF),
            pltpu.VMEM((TOK, 4 * FB), BF),
            pltpu.VMEM((4 * FB, TOK), BF),
            pltpu.VMEM((2, FB, NY * TOK), BF),
            pltpu.VMEM((2, FB // 2, TOK), BF),
            pltpu.VMEM((NY, 4, 8, 128), F32),
            pltpu.VMEM((NZ, 8, 128), F32),
            pltpu.VMEM((8, 8, 128), F32),
            pltpu.VMEM((NY, 8, 128), F32),
            pltpu.VMEM((NZ, 8, 128), F32),
            pltpu.VMEM((NY * TOK, DH), BF),
            pltpu.VMEM((NCH, 2, NZ, ROWS, CH), F32),
            pltpu.VMEM((2, 4, NCH, 2, ROWS, CH), BF),
            pltpu.VMEM((2, 4, NCH, 2, ROWS, CH), BF),
            pltpu.VMEM((NCH, ROWS, CH), F32),
            pltpu.VMEM((2, NCH, ROWS, CH), F32),
            pltpu.SemaphoreType.DMA((20,)),
            pltpu.SemaphoreType.DMA((NSEM,)),
            pltpu.SemaphoreType.DMA((NSEM,)),
        ],
        compiler_params=pltpu.CompilerParams(
            collective_id=0, has_side_effects=True, vmem_limit_bytes=60 * 1024 * 1024,
        ),
    )(hidden_act, readout, weight, log_gap.T, advantage.reshape(1, -1), version.reshape(1, -1),
      lengths, routes.reshape(1, -1))
    lr, grad = pl.pallas_call(
        hand_over,
        out_shape=(
            jax.ShapeDtypeStruct((8, 64), F32),
            jax.ShapeDtypeStruct((ROWS, 2 * DH), F32),
        ),
        in_specs=[vmem, vmem],
        out_specs=(vmem, vmem),
    )(lr, grad)
    return lr.T, grad


def hand_over(lr_in, g_in, lr_out, g_out):
    lr_out[...] = lr_in[...]
    g_out[...] = g_in[...]


def solution(mesh):
    placed = (
        P("dp", "mp"),
        P("dp", None),
        P("dp", None),
        P("dp"),
        P("dp"),
        P("dp", None),
        P("dp", None),
        P(("mp", "dp"), None),
    )
    return jax.shard_map(
        body,
        mesh=mesh,
        in_specs=placed,
        out_specs=(P("dp", None), P(("mp", "dp"), None)),
        check_vma=False,
    )
```

```python
import functools
import math

import jax
import jax.numpy as jnp
from jax import lax
from jax.experimental import pallas as pl
from jax.experimental.pallas import tpu as pltpu
from jax.sharding import PartitionSpec as P

MESH = pl.DeviceIdType.MESH
BF = jnp.bfloat16
F32 = jnp.float32

NX, NY, NZ = 4, 4, 8
TOK = 256
DH = 1280
ROWS = 56
PAIR = 2 * ROWS
FB = ROWS * NZ
FALL = 2 * FB
CHUNKS = tuple((i * 256, 256) for i in range(5))
CH = 256
NCH = len(CHUNKS)
NSEM = 200


def hdot(a, b):
    return lax.dot_general(
        a, b, (((1,), (0,)), ((), ())), precision=lax.Precision.HIGHEST,
        preferred_element_type=F32,
    )


def iota(shape, dim):
    return lax.broadcasted_iota(jnp.int32, shape, dim)


def kernel(scale_out, h_in, r_in, w_in, gap_in, adv_in, ver_in, len_in, route_in,
           lr_out, g_out,
           gap_ref, adv_ref, ver_ref, len_ref, route_ref, lr_buf,
           wbuf, wcat, ubuf, acc, rbuf, hv, htr, ht, relay, pkf, kb, ar1, ar2, lb, og, gbuf,
           rss, rsr, pown, stage, local_sem, send_sem, recv_sem):
    dp = lax.axis_index("dp")
    mp = lax.axis_index("mp")
    y, z = dp // NZ, dp % NZ
    x, c = mp // 2, mp % 2
    px = x % 2
    o = 1 - c
    yp, ym, y2 = (y + 1) % NY, (y + 3) % NY, (y + 2) % NY
    zp, zm = (z + 1) % NZ, (z + 7) % NZ
    xp, xm = (x + 1) % NX, (x + 3) % NX

    def dev(yy, zz, xx, cc):
        return (yy * NZ + zz, xx * 2 + cc)

    d_yp, d_ym, d_y2 = dev(yp, z, x, c), dev(ym, z, x, c), dev(y2, z, x, c)
    d_zp, d_zm = dev(y, zp, x, c), dev(y, zm, x, c)
    d_xp, d_xm = dev(y, z, xp, c), dev(y, z, xm, c)
    d_co = dev(y, z, x, o)
    d_zp_o, d_zm_o = dev(y, zp, x, o), dev(y, zm, x, o)

    count = [0]
    sent = []

    def send(src, dst, where):
        n = count[0]
        count[0] += 1
        copy = pltpu.make_async_remote_copy(
            src_ref=src, dst_ref=dst, send_sem=send_sem.at[n], recv_sem=recv_sem.at[n],
            device_id=where, device_id_type=MESH,
        )
        copy.start()
        sent.append(copy)
        return copy

    half = pl.ds(pl.multiple_of(c * DH, 128), DH)
    other = pl.ds(pl.multiple_of(o * DH, 128), DH)
    mine = pl.ds(pl.multiple_of(y * TOK, TOK), TOK)
    cp_h = pltpu.make_async_copy(h_in, hv, local_sem.at[0])
    cp_h.start()
    cp_r = pltpu.make_async_copy(r_in.at[:, half], rbuf.at[mine, :], local_sem.at[1])
    cp_r.start()
    cp_w = pltpu.make_async_copy(w_in.at[:, half], wbuf.at[c, z], local_sem.at[2])
    cp_w.start()

    small = []
    for i, (a, b) in enumerate((
            (gap_in, gap_ref), (adv_in, adv_ref), (ver_in, ver_ref), (len_in, len_ref),
            (route_in, route_ref))):
        small.append(pltpu.make_async_copy(a, b, local_sem.at[4 + i]))
        small[-1].start()

    far = (z + 4) % NZ

    barrier = pltpu.get_barrier_semaphore()
    chips = [(dp, (mp + k) % 8) for k in range(1, 8)]
    greet = [d_zp, d_zm, d_zp_o, d_zm_o, d_yp, d_ym, d_y2] + chips
    for where in greet:
        pl.semaphore_signal(barrier, inc=1, device_id=where, device_id_type=MESH)
    pl.semaphore_wait(barrier, len(greet))

    W = {}
    WH = DH // 2
    order = ((0, 0), (1, 1), (0, 1), (1, 0))

    def w_first(k, d, h, where):
        first = (c if k == 0 else o) * DH + h * WH
        return send(
            w_in.at[:, pl.ds(pl.multiple_of(first, 128), WH)],
            wbuf.at[c, z, :, h * WH:(h + 1) * WH], where)

    for d, h in order:
        W[0, h, d, 1] = w_first(0, d, h, (d_zp, d_zm)[d])

    hb = px * 128

    def rows_in(part):
        return pl.ds(pl.multiple_of(hb + part * 64, 64), 64)

    def rows_at(yy, part):
        return pl.ds(pl.multiple_of(yy * TOK + hb + part * 64, 64), 64)

    def r_first(part, where):
        return send(r_in.at[rows_in(part), half], rbuf.at[rows_at(y, part), :], where)

    rp_a = r_first(0, d_yp)
    rm_b = r_first(1, d_ym)
    rp_b = r_first(1, d_yp)
    rm_a = r_first(0, d_ym)
    for d, h in order:
        W[1, h, d, 1] = w_first(1, d, h, (d_zp_o, d_zm_o)[d])
    w_co = send(w_in.at[:, other], wbuf.at[c, z], d_co)

    cp_h.wait()
    for j in range(7):
        htr[j * 256:(j + 1) * 256, :] = hv[:, j * 256:(j + 1) * 256].T

    def h_rows(yy, first, rows):
        return pl.ds(pl.multiple_of(yy * FB + first, 32), rows)

    def cols_at(yy):
        return pl.ds(pl.multiple_of(yy * TOK, TOK), TOK)

    cp_ho = pltpu.make_async_copy(
        htr.at[h_rows(y, 0, FB), :], ht.at[c, :, cols_at(y)], local_sem.at[3])
    cp_ho.start()

    for copy in small:
        copy.wait()
    dest_row = route_ref[...].astype(F32)
    ri, ci = iota((32, 32), 0), iota((32, 32), 1)
    dest_col = jnp.sum(
        jnp.where(ri == ci, jnp.broadcast_to(dest_row, (32, 32)), 0.0), axis=1, keepdims=True)
    earlier = jnp.where((dest_col == dest_row) & (ri < ci), 1.0, 0.0)
    rank_row = jnp.sum(earlier, axis=0, keepdims=True)
    key_row = dest_row * 2.0 + rank_row
    ver = ver_ref[...]
    stale_row = jnp.where(
        ver == 3, 1.0, jnp.where(ver == 2, 0.7, jnp.where(ver == 1, 0.7 ** 2, 0.7 ** 3))
    ).astype(F32)
    row8, resp8 = iota((8, 32), 0), iota((8, 32), 1)
    mine8 = (row8 // 2 == y) & (resp8 // 16 == row8 % 2)
    spread = jnp.where(iota((32, 128), 0) % 16 == iota((32, 128), 1) // 8, 1.0, 0.0)

    def lay(v):
        return hdot(jnp.where(mine8, jnp.broadcast_to(v, (8, 32)), 0.0), spread)

    tile = jnp.where(iota((8, 128), 0) == iota((8, 128), 1) % 8, 1.0, 0.0)
    gap_wide = lax.dot_general(
        gap_ref[...], tile, (((0,), (0,)), ((), ())), precision=lax.Precision.HIGHEST,
        preferred_element_type=F32) * spread
    own_rows = iota((8, 128), 0) // 2 == y
    position = (iota((8, 128), 1) % 8).astype(F32)
    len_t = lay(len_ref[...].astype(F32))
    pkf[y, 0] = hdot(jnp.where(mine8, 1.0, 0.0), gap_wide)
    pkf[y, 1] = jnp.where(own_rows & (position >= len_t), -1.0, lay(key_row))
    pkf[y, 2] = lay(adv_ref[...])
    pkf[y, 3] = lay(stale_row)
    len_col = jnp.sum(
        jnp.where(ri == ci, jnp.broadcast_to(len_ref[...].astype(F32), (32, 32)), 0.0),
        axis=1, keepdims=True)
    shard_hit = dest_col == iota((32, 128), 1).astype(F32)
    here = jnp.sum(jnp.where(shard_hit, len_col, 0.0), axis=0, keepdims=True)
    pkf[y, 4] = jnp.broadcast_to(here, (8, 128))
    pk = [send(pkf.at[y], pkf.at[y], d) for d in (d_yp, d_ym, d_y2)]

    def w_forward(k, s):
        core = c if k == 0 else o
        for d, h in order:
            W[k, h, d, s].wait_recv()
            if s == 3 and h != d:
                continue
            origin = (z + (8 - s if d == 0 else s)) % NZ
            cols = slice(h * WH, (h + 1) * WH)
            src = wbuf.at[core, origin, :, cols]
            W[k, h, d, s + 1] = send(src, src, (d_zp, d_zm)[d])

    w_forward(0, 1)

    pairs = [(z // 2 + step) % 4 for step in (0, 1, 3, 2)]

    def build(p, core):
        for n in range(5):
            cols = slice(n * 256, (n + 1) * 256)
            pair = jnp.concatenate(
                [wbuf[core, 2 * pairs[p], :, cols].astype(F32),
                 wbuf[core, 2 * pairs[p] + 1, :, cols].astype(F32)], axis=0)
            wcat[p, core, :, cols] = pair.astype(BF)

    def along(ref_rows, where):
        ref = rbuf.at[ref_rows, :]
        return send(ref, ref, where)

    def piece(yy, part, i):
        first = yy * TOK + hb + part * 64 + i * 32
        return pl.ds(pl.multiple_of(first, 32), 32)

    rp_a.wait_recv()
    r2a = [along(piece(ym, 0, i), d_yp) for i in range(2)]
    xa = [along(rows_at(ym, 0), d_xm)]
    rm_b.wait_recv()
    r2b = [along(piece(yp, 1, i), d_ym) for i in range(2)]
    xb = [along(rows_at(yp, 1), d_xp)]
    h2p = send(htr.at[h_rows(y2, 0, FB // 2), :], relay.at[0], d_yp)
    h2m = send(htr.at[h_rows(y2, FB // 2, FB // 2), :], relay.at[1], d_ym)
    h1 = []
    for first in (0, FB // 2):
        rows = slice(first, first + FB // 2)
        for to, where in ((yp, d_yp), (ym, d_ym)):
            h1.append(send(
                htr.at[h_rows(to, first, FB // 2), :], ht.at[c, rows, cols_at(y)], where))
    cp_ho.wait()
    hp = [send(ht.at[c, :, cols_at(y)], ht.at[c, :, cols_at(y)], d_co)]

    w_forward(1, 1)

    rp_b.wait_recv()
    xb.append(along(rows_at(ym, 1), d_xp))
    rm_a.wait_recv()
    xa.append(along(rows_at(yp, 0), d_xm))

    for copy in pk:
        copy.wait_recv()
    fields = [pkf[0, f] + pkf[1, f] + pkf[2, f] + pkf[3, f] for f in range(5)]
    kb[z, 0] = fields[1]
    kb[z, 1] = fields[4]
    K = {}
    K[0, 1] = send(kb.at[z], kb.at[z], d_zp)
    K[1, 1] = send(kb.at[z], kb.at[z], d_zm)

    def ring_forward(table, buf, s):
        for d, where in ((0, d_zp), (1, d_zm)):
            if (d, s) not in table:
                continue
            table[d, s].wait_recv()
            if s + 1 > (4 if d == 0 else 3):
                continue
            origin = (z + (8 - s if d == 0 else s)) % NZ
            table[d, s + 1] = send(buf.at[origin], buf.at[origin], where)

    cp_w.wait()
    w_co.wait_recv()
    build(0, c)
    build(0, o)
    w_forward(0, 2)
    ring_forward(K, kb, 1)

    for i in range(2):
        r2a[i].wait_recv()
        xa.append(along(piece(y2, 0, i), d_xm))
        r2b[i].wait_recv()
        xb.append(along(piece(y2, 1, i), d_xp))

    w_forward(1, 2)
    ring_forward(K, kb, 2)

    h2p.wait_recv()
    hq_p = send(relay.at[0], ht.at[c, 0:FB // 2, cols_at(ym)], d_yp)
    h2m.wait_recv()
    hq_m = send(relay.at[1], ht.at[c, FB // 2:FB, cols_at(yp)], d_ym)

    w_forward(0, 3)
    build(1, c)
    build(2, c)
    w_forward(1, 3)
    ring_forward(K, kb, 3)

    build(1, o)
    build(2, o)

    def contract(w, r):
        return lax.dot_general(w, r, (((1,), (1,)), ((), ())), preferred_element_type=F32)

    def block(yy):
        ubuf[yy] = contract(
            wcat[0:3].reshape(6 * PAIR, DH),
            rbuf[pl.ds(pl.multiple_of(yy * TOK, TOK), TOK), :])

    def hidden(p, yy):
        rows = pl.ds(pl.multiple_of(pairs[p] * PAIR, 16), PAIR)
        return ht[:, rows, cols_at(yy)].reshape(2 * PAIR, TOK).astype(F32)

    def row_dot(yy):
        total = jnp.zeros((1, TOK), F32)
        for p in range(3):
            u = ubuf[yy, p * 2 * PAIR:(p + 1) * 2 * PAIR, :]
            total = total + jnp.sum(u * hidden(p, yy), axis=0, keepdims=True)
        acc[yy] = total

    for i in range(2):
        rows = slice(i * (FB // 2), (i + 1) * (FB // 2))
        for j, yy in ((0, ym), (1, yp)):
            h1[2 * i + j].wait_recv()
            ref = ht.at[c, rows, cols_at(yy)]
            hp.append(send(ref, ref, d_co))
    cp_r.wait()
    block(y)
    hq_p.wait_recv()
    hq_m.wait_recv()
    hp.append(send(ht.at[c, :, cols_at(y2)], ht.at[c, :, cols_at(y2)], d_co))
    for copy in (xa[0], xb[0], xa[1], xb[1]):
        copy.wait_recv()
    block(ym)
    block(yp)
    for copy in xa[2:] + xb[2:]:
        copy.wait_recv()
    block(y2)
    ring_forward(K, kb, 4)
    for copy in hp[:5]:
        copy.wait_recv()
    row_dot(y)
    row_dot(ym)
    row_dot(yp)
    hp[5].wait_recv()
    row_dot(y2)

    for k, core in ((0, c), (1, o)):
        for d in range(2):
            W[k, d, d, 4].wait_recv()
        build(3, core)
    parts = []
    for b in range(NY):
        u = contract(wcat[3].reshape(2 * PAIR, DH), rbuf[b * TOK:(b + 1) * TOK, :])
        s = acc[b] + jnp.sum(u * hidden(3, b), axis=0, keepdims=True)
        parts += [s[:, 0:128], s[:, 128:256]]
    ar1[mp] = jnp.concatenate(parts, axis=0)
    partial = [send(ar1.at[mp], ar1.at[mp], where) for where in chips]

    tally = kb[0, 1]
    for i in range(1, NZ):
        tally = tally + kb[i, 1]
    own_dest = jnp.floor(fields[1] * 0.5)
    count_each = jnp.ones((8, 128), F32)
    for k in range(NY * NZ):
        count_each = jnp.where(own_dest == float(k), tally[:, k:k + 1], count_each)

    for copy in partial:
        copy.wait_recv()
    ar2[y] = ((ar1[0] + ar1[1]) + (ar1[2] + ar1[3])) + ((ar1[4] + ar1[5]) + (ar1[6] + ar1[7]))
    partial = [send(ar2.at[y], ar2.at[y], where) for where in (d_yp, d_ym, d_y2)]
    for copy in partial:
        copy.wait_recv()
    total = (ar2[0] + ar2[1]) + (ar2[2] + ar2[3])

    gap, key, adv, stale = fields[:4]
    live = key >= 0.0
    logit = gap + total * scale_out
    lb[z] = jnp.where(live, logit, 0.0)
    ratio = jnp.exp(logit)
    squash = jnp.tanh((ratio - 1.0) / 0.2)
    clipped = 1.0 + 0.2 * squash
    plain = ratio * adv <= clipped * adv
    slope = jnp.where(plain, 1.0, 1.0 - squash * squash)
    coef = jnp.where(live, -512.0 * stale * adv * ratio * slope / count_each, 0.0)
    coef_col = (coef * scale_out).T

    RS = {}

    ends = ((0, d_zp), (1, d_zm))
    hall = ht[...].reshape(FALL, NY * TOK)
    for n, (start, wide) in enumerate(CHUNKS):
        cols = slice(start, start + wide)
        for b in range(8):
            rows = slice(b * 128, (b + 1) * 128)
            og[rows, cols] = (coef_col[:, b:b + 1] * rbuf[rows, cols].astype(F32)).astype(BF)
        g = jnp.dot(hall, og[:, cols], preferred_element_type=F32)
        w = slice(0, wide)
        gbuf[n, :, :, :, w] = g.reshape(2, NZ, ROWS, wide)
        for d, where in ends:
            rss[d, 0, n, d, :, w] = gbuf[n, d, far, :, w].astype(BF)
            RS[d, 1, n] = send(rss.at[d, 0, n, d, :, w], rsr.at[d, 0, n, d, :, w], where)
    shares = [
        send(gbuf.at[n, o, z, :, 0:CHUNKS[n][1]], pown.at[n, :, 0:CHUNKS[n][1]], d_co)
        for n in range(NCH)
    ]

    L = {}
    L[0, 1] = send(lb.at[z], lb.at[z], d_zp)
    L[1, 1] = send(lb.at[z], lb.at[z], d_zm)

    for s in range(2, 5):
        for n, (start, wide) in enumerate(CHUNKS):
            w = slice(0, wide)
            for d, where in ends:
                to = (z + (5 - s if d == 0 else 3 + s)) % NZ
                RS[d, s - 1, n].wait_recv()
                if s == 2:
                    rss[d, 1, n, d, :, w] = (
                        gbuf[n, d, to, :, w] + rsr[d, 0, n, d, :, w].astype(F32)).astype(BF)
                    rss[d, 1, n, 1 - d, :, w] = gbuf[n, 1 - d, to, :, w].astype(BF)
                else:
                    rss[d, s - 1, n, :, :, w] = (
                        gbuf[n, :, to, :, w] + rsr[d, s - 2, n, :, :, w].astype(F32)).astype(BF)
                if s < 4:
                    RS[d, s, n] = send(
                        rss.at[d, s - 1, n, :, :, w], rsr.at[d, s - 1, n, :, :, w], where)
                else:
                    RS[d, 4, n] = [
                        send(rss.at[d, 3, n, c, :, w], rsr.at[d, 3, n, 0, :, w], where),
                        send(rss.at[d, 3, n, o, :, w], rsr.at[d, 3, n, 1, :, w],
                             (d_zp_o, d_zm_o)[d]),
                    ]
        ring_forward(L, lb, s - 1)

    ring_forward(L, lb, 4)
    key_all = kb[:, 0].reshape(64, 128)
    val_all = lb[...].reshape(64, 128)
    fold = jnp.where(iota((128, 8), 0) % 8 == iota((128, 8), 1), 1.0, 0.0)
    oi, ki = iota((64, 64), 0), iota((64, 64), 1)
    source = ((ki % 8) // 2) * NZ + ki // 8
    out = jnp.zeros((64, 8), F32)
    for r in range(2):
        want = (2 * dp + r).astype(F32)
        v = hdot(jnp.where(key_all == want, val_all, 0.0), fold)
        out = out + hdot(jnp.where(oi == 2 * source + r, 1.0, 0.0), v)
    lr_buf[...] = out.T
    outs = [pltpu.make_async_copy(lr_buf, lr_out, local_sem.at[9])]
    outs[0].start()

    for n, (start, wide) in enumerate(CHUNKS):
        w = slice(0, wide)
        shares[n].wait_recv()
        for d, _ in ends:
            for copy in RS[d, 4, n]:
                copy.wait_recv()
        for i, (core, own) in enumerate(((c, gbuf[n, c, z, :, w]), (o, pown[n, :, w]))):
            stage[i, n, :, w] = (
                own + rsr[0, 3, n, i, :, w].astype(F32) + rsr[1, 3, n, i, :, w].astype(F32))
            cols = pl.ds(pl.multiple_of(core * DH + start, 128), wide)
            out = pltpu.make_async_copy(
                stage.at[i, n, :, w], g_out.at[:, cols], local_sem.at[10 + 2 * n + i])
            out.start()
            outs.append(out)

    for copy in outs:
        copy.wait()
    for copy in sent:
        copy.wait_send()
    assert count[0] <= NSEM, count[0]


def body(hidden_act, readout, log_gap, advantage, version, lengths, routes, weight):
    width = readout.shape[1]
    any_spec = pl.BlockSpec(memory_space=pl.ANY)
    vmem = pl.BlockSpec(memory_space=pltpu.VMEM)
    lr, grad = pl.pallas_call(
        functools.partial(kernel, 0.15 / math.sqrt(width)),
        out_shape=(
            jax.ShapeDtypeStruct((8, 64), F32),
            jax.ShapeDtypeStruct((ROWS, 2 * DH), F32),
        ),
        in_specs=[any_spec] * 8,
        out_specs=(any_spec, any_spec),
        scratch_shapes=[
            pltpu.VMEM((8, 32), F32),
            pltpu.VMEM((1, 32), F32),
            pltpu.VMEM((1, 32), jnp.int32),
            pltpu.VMEM((1, 32), jnp.int32),
            pltpu.VMEM((1, 32), jnp.int32),
            pltpu.VMEM((8, 64), F32),
            pltpu.VMEM((2, NZ, ROWS, DH), BF),
            pltpu.VMEM((4, 2, PAIR, DH), BF),
            pltpu.VMEM((NY, 6 * PAIR, TOK), F32),
            pltpu.VMEM((NY, 1, TOK), F32),
            pltpu.VMEM((NY * TOK, DH), BF),
            pltpu.VMEM((TOK, 4 * FB), BF),
            pltpu.VMEM((4 * FB, TOK), BF),
            pltpu.VMEM((2, FB, NY * TOK), BF),
            pltpu.VMEM((2, FB // 2, TOK), BF),
            pltpu.VMEM((NY, 5, 8, 128), F32),
            pltpu.VMEM((NZ, 2, 8, 128), F32),
            pltpu.VMEM((8, 8, 128), F32),
            pltpu.VMEM((NY, 8, 128), F32),
            pltpu.VMEM((NZ, 8, 128), F32),
            pltpu.VMEM((NY * TOK, DH), BF),
            pltpu.VMEM((NCH, 2, NZ, ROWS, CH), F32),
            pltpu.VMEM((2, 4, NCH, 2, ROWS, CH), BF),
            pltpu.VMEM((2, 4, NCH, 2, ROWS, CH), BF),
            pltpu.VMEM((NCH, ROWS, CH), F32),
            pltpu.VMEM((2, NCH, ROWS, CH), F32),
            pltpu.SemaphoreType.DMA((10 + 2 * NCH,)),
            pltpu.SemaphoreType.DMA((NSEM,)),
            pltpu.SemaphoreType.DMA((NSEM,)),
        ],
        compiler_params=pltpu.CompilerParams(
            collective_id=0, has_side_effects=True, vmem_limit_bytes=60 * 1024 * 1024,
        ),
    )(hidden_act, readout, weight, log_gap.T, advantage.reshape(1, -1), version.reshape(1, -1),
      lengths, routes.reshape(1, -1))
    lr, grad = pl.pallas_call(
        hand_over,
        out_shape=(
            jax.ShapeDtypeStruct((8, 64), F32),
            jax.ShapeDtypeStruct((ROWS, 2 * DH), F32),
        ),
        in_specs=[vmem, vmem],
        out_specs=(vmem, vmem),
    )(lr, grad)
    return lr.T, grad


def hand_over(lr_in, g_in, lr_out, g_out):
    lr_out[...] = lr_in[...]
    g_out[...] = g_in[...]


def solution(mesh):
    placed = (
        P("dp", "mp"),
        P("dp", None),
        P("dp", None),
        P("dp"),
        P("dp"),
        P("dp", None),
        P("dp", None),
        P(("mp", "dp"), None),
    )
    return jax.shard_map(
        body,
        mesh=mesh,
        in_specs=placed,
        out_specs=(P("dp", None), P(("mp", "dp"), None)),
        check_vma=False,
    )
```

```python
import functools
import math

import jax
import jax.numpy as jnp
from jax import lax
from jax.experimental import pallas as pl
from jax.experimental.pallas import tpu as pltpu
from jax.sharding import PartitionSpec as P

MESH = pl.DeviceIdType.MESH
BF = jnp.bfloat16
F32 = jnp.float32

NX, NY, NZ = 4, 4, 8
TOK = 256
DH = 1280
ROWS = 56
PAIR = 2 * ROWS
FB = ROWS * NZ
FALL = 2 * FB
CHUNKS = ((0, 384), (384, 512), (896, 384))
CH = 512
NCH = len(CHUNKS)
NSEM = 200


def hdot(a, b):
    return lax.dot_general(
        a, b, (((1,), (0,)), ((), ())), precision=lax.Precision.HIGHEST,
        preferred_element_type=F32,
    )


def iota(shape, dim):
    return lax.broadcasted_iota(jnp.int32, shape, dim)


def kernel(scale_out, h_in, r_in, w_in, gap_in, adv_in, ver_in, len_in, route_in,
           lr_out, g_out,
           gap_ref, adv_ref, ver_ref, len_ref, route_ref, lr_buf,
           wbuf, wcat, ubuf, acc, rbuf, hv, htr, ht, relay, pkf, kb, ar1, ar2, lb, og, gbuf,
           rss, rsr, pown, stage, local_sem, send_sem, recv_sem):
    dp = lax.axis_index("dp")
    mp = lax.axis_index("mp")
    y, z = dp // NZ, dp % NZ
    x, c = mp // 2, mp % 2
    px = x % 2
    o = 1 - c
    yp, ym, y2 = (y + 1) % NY, (y + 3) % NY, (y + 2) % NY
    zp, zm = (z + 1) % NZ, (z + 7) % NZ
    xp, xm = (x + 1) % NX, (x + 3) % NX

    def dev(yy, zz, xx, cc):
        return (yy * NZ + zz, xx * 2 + cc)

    d_yp, d_ym, d_y2 = dev(yp, z, x, c), dev(ym, z, x, c), dev(y2, z, x, c)
    d_zp, d_zm = dev(y, zp, x, c), dev(y, zm, x, c)
    d_xp, d_xm = dev(y, z, xp, c), dev(y, z, xm, c)
    d_co = dev(y, z, x, o)
    d_zp_o, d_zm_o = dev(y, zp, x, o), dev(y, zm, x, o)

    count = [0]
    sent = []

    def send(src, dst, where):
        n = count[0]
        count[0] += 1
        copy = pltpu.make_async_remote_copy(
            src_ref=src, dst_ref=dst, send_sem=send_sem.at[n], recv_sem=recv_sem.at[n],
            device_id=where, device_id_type=MESH,
        )
        copy.start()
        sent.append(copy)
        return copy

    half = pl.ds(pl.multiple_of(c * DH, 128), DH)
    other = pl.ds(pl.multiple_of(o * DH, 128), DH)
    mine = pl.ds(pl.multiple_of(y * TOK, TOK), TOK)
    cp_h = pltpu.make_async_copy(h_in, hv, local_sem.at[0])
    cp_h.start()
    cp_r = pltpu.make_async_copy(r_in.at[:, half], rbuf.at[mine, :], local_sem.at[1])
    cp_r.start()
    cp_w = pltpu.make_async_copy(w_in.at[:, half], wbuf.at[c, z], local_sem.at[2])
    cp_w.start()

    small = []
    for i, (a, b) in enumerate((
            (gap_in, gap_ref), (adv_in, adv_ref), (ver_in, ver_ref), (len_in, len_ref),
            (route_in, route_ref))):
        small.append(pltpu.make_async_copy(a, b, local_sem.at[4 + i]))
        small[-1].start()

    far = (z + 4) % NZ

    barrier = pltpu.get_barrier_semaphore()
    chips = [(dp, (mp + k) % 8) for k in range(1, 8)]
    greet = [d_zp, d_zm, d_zp_o, d_zm_o, d_yp, d_ym, d_y2] + chips
    for where in greet:
        pl.semaphore_signal(barrier, inc=1, device_id=where, device_id_type=MESH)
    pl.semaphore_wait(barrier, len(greet))

    W = {}
    WH = DH // 2
    order = ((0, 0), (1, 1), (0, 1), (1, 0))

    def w_first(k, d, h, where):
        first = (c if k == 0 else o) * DH + h * WH
        return send(
            w_in.at[:, pl.ds(pl.multiple_of(first, 128), WH)],
            wbuf.at[c, z, :, h * WH:(h + 1) * WH], where)

    for d, h in order:
        W[0, h, d, 1] = w_first(0, d, h, (d_zp, d_zm)[d])

    hb = px * 128

    def rows_in(part):
        return pl.ds(pl.multiple_of(hb + part * 64, 64), 64)

    def rows_at(yy, part):
        return pl.ds(pl.multiple_of(yy * TOK + hb + part * 64, 64), 64)

    def r_first(part, where):
        return send(r_in.at[rows_in(part), half], rbuf.at[rows_at(y, part), :], where)

    rp_a = r_first(0, d_yp)
    rm_b = r_first(1, d_ym)
    rp_b = r_first(1, d_yp)
    rm_a = r_first(0, d_ym)
    for d, h in order:
        W[1, h, d, 1] = w_first(1, d, h, (d_zp_o, d_zm_o)[d])
    w_co = send(w_in.at[:, other], wbuf.at[c, z], d_co)

    cp_h.wait()
    for j in range(7):
        htr[j * 256:(j + 1) * 256, :] = hv[:, j * 256:(j + 1) * 256].T

    def h_rows(yy, first, rows):
        return pl.ds(pl.multiple_of(yy * FB + first, 32), rows)

    def cols_at(yy):
        return pl.ds(pl.multiple_of(yy * TOK, TOK), TOK)

    cp_ho = pltpu.make_async_copy(
        htr.at[h_rows(y, 0, FB), :], ht.at[c, :, cols_at(y)], local_sem.at[3])
    cp_ho.start()

    for copy in small:
        copy.wait()
    dest_row = route_ref[...].astype(F32)
    ri, ci = iota((32, 32), 0), iota((32, 32), 1)
    dest_col = jnp.sum(
        jnp.where(ri == ci, jnp.broadcast_to(dest_row, (32, 32)), 0.0), axis=1, keepdims=True)
    earlier = jnp.where((dest_col == dest_row) & (ri < ci), 1.0, 0.0)
    rank_row = jnp.sum(earlier, axis=0, keepdims=True)
    key_row = dest_row * 2.0 + rank_row
    ver = ver_ref[...]
    stale_row = jnp.where(
        ver == 3, 1.0, jnp.where(ver == 2, 0.7, jnp.where(ver == 1, 0.7 ** 2, 0.7 ** 3))
    ).astype(F32)
    row8, resp8 = iota((8, 32), 0), iota((8, 32), 1)
    mine8 = (row8 // 2 == y) & (resp8 // 16 == row8 % 2)
    spread = jnp.where(iota((32, 128), 0) % 16 == iota((32, 128), 1) // 8, 1.0, 0.0)

    def lay(v):
        return hdot(jnp.where(mine8, jnp.broadcast_to(v, (8, 32)), 0.0), spread)

    tile = jnp.where(iota((8, 128), 0) == iota((8, 128), 1) % 8, 1.0, 0.0)
    gap_wide = lax.dot_general(
        gap_ref[...], tile, (((0,), (0,)), ((), ())), precision=lax.Precision.HIGHEST,
        preferred_element_type=F32) * spread
    own_rows = iota((8, 128), 0) // 2 == y
    position = (iota((8, 128), 1) % 8).astype(F32)
    len_t = lay(len_ref[...].astype(F32))
    pkf[y, 0] = hdot(jnp.where(mine8, 1.0, 0.0), gap_wide)
    pkf[y, 1] = jnp.where(own_rows & (position >= len_t), -1.0, lay(key_row))
    pkf[y, 2] = lay(adv_ref[...])
    pkf[y, 3] = lay(stale_row)
    len_col = jnp.sum(
        jnp.where(ri == ci, jnp.broadcast_to(len_ref[...].astype(F32), (32, 32)), 0.0),
        axis=1, keepdims=True)
    shard_hit = dest_col == iota((32, 128), 1).astype(F32)
    here = jnp.sum(jnp.where(shard_hit, len_col, 0.0), axis=0, keepdims=True)
    pkf[y, 4] = jnp.broadcast_to(here, (8, 128))
    pk = [send(pkf.at[y], pkf.at[y], d) for d in (d_yp, d_ym, d_y2)]

    def w_forward(k, s):
        core = c if k == 0 else o
        for d, h in order:
            W[k, h, d, s].wait_recv()
            if s == 3 and h != d:
                continue
            origin = (z + (8 - s if d == 0 else s)) % NZ
            cols = slice(h * WH, (h + 1) * WH)
            src = wbuf.at[core, origin, :, cols]
            W[k, h, d, s + 1] = send(src, src, (d_zp, d_zm)[d])

    w_forward(0, 1)

    pairs = [(z // 2 + step) % 4 for step in (0, 1, 3, 2)]

    def build(p, core):
        for n in range(5):
            cols = slice(n * 256, (n + 1) * 256)
            pair = jnp.concatenate(
                [wbuf[core, 2 * pairs[p], :, cols].astype(F32),
                 wbuf[core, 2 * pairs[p] + 1, :, cols].astype(F32)], axis=0)
            wcat[p, core, :, cols] = pair.astype(BF)

    def along(ref_rows, where):
        ref = rbuf.at[ref_rows, :]
        return send(ref, ref, where)

    def piece(yy, part, i):
        first = yy * TOK + hb + part * 64 + i * 32
        return pl.ds(pl.multiple_of(first, 32), 32)

    rp_a.wait_recv()
    r2a = [along(piece(ym, 0, i), d_yp) for i in range(2)]
    xa = [along(rows_at(ym, 0), d_xm)]
    rm_b.wait_recv()
    r2b = [along(piece(yp, 1, i), d_ym) for i in range(2)]
    xb = [along(rows_at(yp, 1), d_xp)]
    h2p = send(htr.at[h_rows(y2, 0, FB // 2), :], relay.at[0], d_yp)
    h2m = send(htr.at[h_rows(y2, FB // 2, FB // 2), :], relay.at[1], d_ym)
    h1 = []
    for first in (0, FB // 2):
        rows = slice(first, first + FB // 2)
        for to, where in ((yp, d_yp), (ym, d_ym)):
            h1.append(send(
                htr.at[h_rows(to, first, FB // 2), :], ht.at[c, rows, cols_at(y)], where))
    cp_ho.wait()
    hp = [send(ht.at[c, :, cols_at(y)], ht.at[c, :, cols_at(y)], d_co)]

    w_forward(1, 1)

    rp_b.wait_recv()
    xb.append(along(rows_at(ym, 1), d_xp))
    rm_a.wait_recv()
    xa.append(along(rows_at(yp, 0), d_xm))

    for copy in pk:
        copy.wait_recv()
    fields = [pkf[0, f] + pkf[1, f] + pkf[2, f] + pkf[3, f] for f in range(5)]
    kb[z, 0] = fields[1]
    kb[z, 1] = fields[4]
    K = {}
    K[0, 1] = send(kb.at[z], kb.at[z], d_zp)
    K[1, 1] = send(kb.at[z], kb.at[z], d_zm)

    def ring_forward(table, buf, s):
        for d, where in ((0, d_zp), (1, d_zm)):
            if (d, s) not in table:
                continue
            table[d, s].wait_recv()
            if s + 1 > (4 if d == 0 else 3):
                continue
            origin = (z + (8 - s if d == 0 else s)) % NZ
            table[d, s + 1] = send(buf.at[origin], buf.at[origin], where)

    cp_w.wait()
    w_co.wait_recv()
    build(0, c)
    build(0, o)
    w_forward(0, 2)
    ring_forward(K, kb, 1)

    for i in range(2):
        r2a[i].wait_recv()
        xa.append(along(piece(y2, 0, i), d_xm))
        r2b[i].wait_recv()
        xb.append(along(piece(y2, 1, i), d_xp))

    w_forward(1, 2)
    ring_forward(K, kb, 2)

    h2p.wait_recv()
    hq_p = send(relay.at[0], ht.at[c, 0:FB // 2, cols_at(ym)], d_yp)
    h2m.wait_recv()
    hq_m = send(relay.at[1], ht.at[c, FB // 2:FB, cols_at(yp)], d_ym)

    w_forward(0, 3)
    build(1, c)
    build(2, c)
    w_forward(1, 3)
    ring_forward(K, kb, 3)

    build(1, o)
    build(2, o)

    def contract(w, r):
        return lax.dot_general(w, r, (((1,), (1,)), ((), ())), preferred_element_type=F32)

    def block(yy):
        ubuf[yy] = contract(
            wcat[0:3].reshape(6 * PAIR, DH),
            rbuf[pl.ds(pl.multiple_of(yy * TOK, TOK), TOK), :])

    def hidden(p, yy):
        rows = pl.ds(pl.multiple_of(pairs[p] * PAIR, 16), PAIR)
        return ht[:, rows, cols_at(yy)].reshape(2 * PAIR, TOK).astype(F32)

    def row_dot(yy):
        total = jnp.zeros((1, TOK), F32)
        for p in range(3):
            u = ubuf[yy, p * 2 * PAIR:(p + 1) * 2 * PAIR, :]
            total = total + jnp.sum(u * hidden(p, yy), axis=0, keepdims=True)
        acc[yy] = total

    for i in range(2):
        rows = slice(i * (FB // 2), (i + 1) * (FB // 2))
        for j, yy in ((0, ym), (1, yp)):
            h1[2 * i + j].wait_recv()
            ref = ht.at[c, rows, cols_at(yy)]
            hp.append(send(ref, ref, d_co))
    cp_r.wait()
    block(y)
    hq_p.wait_recv()
    hq_m.wait_recv()
    hp.append(send(ht.at[c, :, cols_at(y2)], ht.at[c, :, cols_at(y2)], d_co))
    for copy in (xa[0], xb[0], xa[1], xb[1]):
        copy.wait_recv()
    block(ym)
    block(yp)
    for copy in xa[2:] + xb[2:]:
        copy.wait_recv()
    block(y2)
    ring_forward(K, kb, 4)
    for copy in hp[:5]:
        copy.wait_recv()
    row_dot(y)
    row_dot(ym)
    row_dot(yp)
    hp[5].wait_recv()
    row_dot(y2)

    for k, core in ((0, c), (1, o)):
        for d in range(2):
            W[k, d, d, 4].wait_recv()
        build(3, core)
    parts = []
    for b in range(NY):
        u = contract(wcat[3].reshape(2 * PAIR, DH), rbuf[b * TOK:(b + 1) * TOK, :])
        s = acc[b] + jnp.sum(u * hidden(3, b), axis=0, keepdims=True)
        parts += [s[:, 0:128], s[:, 128:256]]
    ar1[mp] = jnp.concatenate(parts, axis=0)
    partial = [send(ar1.at[mp], ar1.at[mp], where) for where in chips]

    tally = kb[0, 1]
    for i in range(1, NZ):
        tally = tally + kb[i, 1]
    own_dest = jnp.floor(fields[1] * 0.5)
    count_each = jnp.ones((8, 128), F32)
    for k in range(NY * NZ):
        count_each = jnp.where(own_dest == float(k), tally[:, k:k + 1], count_each)

    for copy in partial:
        copy.wait_recv()
    ar2[y] = ((ar1[0] + ar1[1]) + (ar1[2] + ar1[3])) + ((ar1[4] + ar1[5]) + (ar1[6] + ar1[7]))
    partial = [send(ar2.at[y], ar2.at[y], where) for where in (d_yp, d_ym, d_y2)]
    for copy in partial:
        copy.wait_recv()
    total = (ar2[0] + ar2[1]) + (ar2[2] + ar2[3])

    gap, key, adv, stale = fields[:4]
    live = key >= 0.0
    logit = gap + total * scale_out
    lb[z] = jnp.where(live, logit, 0.0)
    ratio = jnp.exp(logit)
    squash = jnp.tanh((ratio - 1.0) / 0.2)
    clipped = 1.0 + 0.2 * squash
    plain = ratio * adv <= clipped * adv
    slope = jnp.where(plain, 1.0, 1.0 - squash * squash)
    coef = jnp.where(live, -512.0 * stale * adv * ratio * slope / count_each, 0.0)
    coef_col = (coef * scale_out).T

    RS = {}

    ends = ((0, d_zp), (1, d_zm))
    hall = ht[...].reshape(FALL, NY * TOK)
    for n, (start, wide) in enumerate(CHUNKS):
        cols = slice(start, start + wide)
        for b in range(8):
            rows = slice(b * 128, (b + 1) * 128)
            og[rows, cols] = (coef_col[:, b:b + 1] * rbuf[rows, cols].astype(F32)).astype(BF)
        g = jnp.dot(hall, og[:, cols], preferred_element_type=F32)
        w = slice(0, wide)
        gbuf[n, :, :, :, w] = g.reshape(2, NZ, ROWS, wide)
        for d, where in ends:
            rss[d, 0, n, d, :, w] = gbuf[n, d, far, :, w].astype(BF)
            RS[d, 1, n] = send(rss.at[d, 0, n, d, :, w], rsr.at[d, 0, n, d, :, w], where)
    shares = [
        send(gbuf.at[n, o, z, :, 0:CHUNKS[n][1]], pown.at[n, :, 0:CHUNKS[n][1]], d_co)
        for n in range(NCH)
    ]

    L = {}
    L[0, 1] = send(lb.at[z], lb.at[z], d_zp)
    L[1, 1] = send(lb.at[z], lb.at[z], d_zm)

    for s in range(2, 5):
        for n, (start, wide) in enumerate(CHUNKS):
            w = slice(0, wide)
            for d, where in ends:
                to = (z + (5 - s if d == 0 else 3 + s)) % NZ
                RS[d, s - 1, n].wait_recv()
                if s == 2:
                    rss[d, 1, n, d, :, w] = (
                        gbuf[n, d, to, :, w] + rsr[d, 0, n, d, :, w].astype(F32)).astype(BF)
                    rss[d, 1, n, 1 - d, :, w] = gbuf[n, 1 - d, to, :, w].astype(BF)
                else:
                    rss[d, s - 1, n, :, :, w] = (
                        gbuf[n, :, to, :, w] + rsr[d, s - 2, n, :, :, w].astype(F32)).astype(BF)
                if s < 4:
                    RS[d, s, n] = send(
                        rss.at[d, s - 1, n, :, :, w], rsr.at[d, s - 1, n, :, :, w], where)
                else:
                    RS[d, 4, n] = [
                        send(rss.at[d, 3, n, c, :, w], rsr.at[d, 3, n, 0, :, w], where),
                        send(rss.at[d, 3, n, o, :, w], rsr.at[d, 3, n, 1, :, w],
                             (d_zp_o, d_zm_o)[d]),
                    ]
        ring_forward(L, lb, s - 1)

    ring_forward(L, lb, 4)
    key_all = kb[:, 0].reshape(64, 128)
    val_all = lb[...].reshape(64, 128)
    fold = jnp.where(iota((128, 8), 0) % 8 == iota((128, 8), 1), 1.0, 0.0)
    oi, ki = iota((64, 64), 0), iota((64, 64), 1)
    source = ((ki % 8) // 2) * NZ + ki // 8
    out = jnp.zeros((64, 8), F32)
    for r in range(2):
        want = (2 * dp + r).astype(F32)
        v = hdot(jnp.where(key_all == want, val_all, 0.0), fold)
        out = out + hdot(jnp.where(oi == 2 * source + r, 1.0, 0.0), v)
    lr_buf[...] = out.T
    outs = [pltpu.make_async_copy(lr_buf, lr_out, local_sem.at[9])]
    outs[0].start()

    for n, (start, wide) in enumerate(CHUNKS):
        w = slice(0, wide)
        shares[n].wait_recv()
        for d, _ in ends:
            for copy in RS[d, 4, n]:
                copy.wait_recv()
        for i, (core, own) in enumerate(((c, gbuf[n, c, z, :, w]), (o, pown[n, :, w]))):
            stage[i, n, :, w] = (
                own + rsr[0, 3, n, i, :, w].astype(F32) + rsr[1, 3, n, i, :, w].astype(F32))
            cols = pl.ds(pl.multiple_of(core * DH + start, 128), wide)
            out = pltpu.make_async_copy(
                stage.at[i, n, :, w], g_out.at[:, cols], local_sem.at[10 + 2 * n + i])
            out.start()
            outs.append(out)

    for copy in outs:
        copy.wait()
    for copy in sent:
        copy.wait_send()
    assert count[0] <= NSEM, count[0]


def body(hidden_act, readout, log_gap, advantage, version, lengths, routes, weight):
    width = readout.shape[1]
    any_spec = pl.BlockSpec(memory_space=pl.ANY)
    vmem = pl.BlockSpec(memory_space=pltpu.VMEM)
    lr, grad = pl.pallas_call(
        functools.partial(kernel, 0.15 / math.sqrt(width)),
        out_shape=(
            jax.ShapeDtypeStruct((8, 64), F32),
            jax.ShapeDtypeStruct((ROWS, 2 * DH), F32),
        ),
        in_specs=[any_spec] * 8,
        out_specs=(any_spec, any_spec),
        scratch_shapes=[
            pltpu.VMEM((8, 32), F32),
            pltpu.VMEM((1, 32), F32),
            pltpu.VMEM((1, 32), jnp.int32),
            pltpu.VMEM((1, 32), jnp.int32),
            pltpu.VMEM((1, 32), jnp.int32),
            pltpu.VMEM((8, 64), F32),
            pltpu.VMEM((2, NZ, ROWS, DH), BF),
            pltpu.VMEM((4, 2, PAIR, DH), BF),
            pltpu.VMEM((NY, 6 * PAIR, TOK), F32),
            pltpu.VMEM((NY, 1, TOK), F32),
            pltpu.VMEM((NY * TOK, DH), BF),
            pltpu.VMEM((TOK, 4 * FB), BF),
            pltpu.VMEM((4 * FB, TOK), BF),
            pltpu.VMEM((2, FB, NY * TOK), BF),
            pltpu.VMEM((2, FB // 2, TOK), BF),
            pltpu.VMEM((NY, 5, 8, 128), F32),
            pltpu.VMEM((NZ, 2, 8, 128), F32),
            pltpu.VMEM((8, 8, 128), F32),
            pltpu.VMEM((NY, 8, 128), F32),
            pltpu.VMEM((NZ, 8, 128), F32),
            pltpu.VMEM((NY * TOK, DH), BF),
            pltpu.VMEM((NCH, 2, NZ, ROWS, CH), F32),
            pltpu.VMEM((2, 4, NCH, 2, ROWS, CH), BF),
            pltpu.VMEM((2, 4, NCH, 2, ROWS, CH), BF),
            pltpu.VMEM((NCH, ROWS, CH), F32),
            pltpu.VMEM((2, NCH, ROWS, CH), F32),
            pltpu.SemaphoreType.DMA((10 + 2 * NCH,)),
            pltpu.SemaphoreType.DMA((NSEM,)),
            pltpu.SemaphoreType.DMA((NSEM,)),
        ],
        compiler_params=pltpu.CompilerParams(
            collective_id=0, has_side_effects=True, vmem_limit_bytes=60 * 1024 * 1024,
        ),
    )(hidden_act, readout, weight, log_gap.T, advantage.reshape(1, -1), version.reshape(1, -1),
      lengths, routes.reshape(1, -1))
    lr, grad = pl.pallas_call(
        hand_over,
        out_shape=(
            jax.ShapeDtypeStruct((8, 64), F32),
            jax.ShapeDtypeStruct((ROWS, 2 * DH), F32),
        ),
        in_specs=[vmem, vmem],
        out_specs=(vmem, vmem),
    )(lr, grad)
    return lr.T, grad


def hand_over(lr_in, g_in, lr_out, g_out):
    lr_out[...] = lr_in[...]
    g_out[...] = g_in[...]


def solution(mesh):
    placed = (
        P("dp", "mp"),
        P("dp", None),
        P("dp", None),
        P("dp"),
        P("dp"),
        P("dp", None),
        P("dp", None),
        P(("mp", "dp"), None),
    )
    return jax.shard_map(
        body,
        mesh=mesh,
        in_specs=placed,
        out_specs=(P("dp", None), P(("mp", "dp"), None)),
        check_vma=False,
    )
```
